32 devices in a mesh: radial: 8 (over y, x, core), mode: 4 (over z).
Axes of the slice: x: 2, y: 2, z: 4, core: 2. Of those that a mesh axis runs over, the one named last changes fastest.
Arguments:
- scalar_field: float32 [256, 64, 2, 384], P('radial', 'mode'), may hold values from -48 to 48
- radial_flow: float32 [256, 64, 2, 384], P('radial', 'mode'), may hold values from -6 to 6
- legendre: bfloat16 [64, 384, 768], P('mode'), may hold values from -0.3125 to 0.3125
- diffusivity: float32 [256], P('radial'), may hold values from 1000 to 100000
Outputs:
- field_new: float32 [256, 64, 2, 384], P('radial', 'mode')
The draws below stay inside these ranges and needn't reach their ends.
All inputs are finite; a program needn't handle non-finite values.
Results may differ from the reference program's by a relative error of at most 0.0071.
Values may be sent and summed in bfloat16 or wider, within the bound.
A program may use at most 128 MiB of HBM per device.

```python
import math
import jax
import jax.numpy as jnp
from jax import lax

DEG = 384
NLAT = 768
NLON = 1536
NR = 256
ORDERS = 64
ROFF = 137


def shard_levels(key, dims, cuts, smallest, high):
    gain = 1.0
    for dim, parts in cuts:
        draws = jax.random.uniform(jax.random.fold_in(jax.random.fold_in(key, 6), dim), (parts,), jnp.float32, smallest / len(cuts), high / len(cuts))
        gain = gain * jnp.repeat(jnp.exp(draws), dims[dim] // parts).reshape((-1,) + (1,) * (len(dims) - 1 - dim))
    return gain


def normal_values(stream_key, dims, width, reach, split=(), held_as=jnp.bfloat16):
    drawn = jax.random.normal(stream_key, dims, jnp.float32) * width
    if len(split) > 0:
        drawn = shard_levels(stream_key, dims, split, -0.22, 0.18) * drawn
    return jnp.clip(drawn, min=-reach, max=reach).astype(held_as)


def setup_inputs(seed: int = 0) -> dict:
    seeds = jax.random.split(jax.random.key(seed), 5)
    return {
        "scalar_field": normal_values(seeds[0], (NR, ORDERS, 2, DEG), 8.0, 48.0, ((0, 8), (1, 4)), jnp.float32),
        "radial_flow": normal_values(seeds[1], (NR, ORDERS, 2, DEG), 1.0, 6.0, ((0, 8), (1, 4)), jnp.float32),
        "legendre": normal_values(seeds[2], (ORDERS, DEG, NLAT), DEG ** -0.5, 0.3125, ((0, 4),)),
        "diffusivity": jnp.clip(jnp.exp(math.log(100000.0) - 4.6051702 * jax.random.uniform(seeds[3], (NR,), jnp.float32) ** shard_levels(seeds[3], (NR,), ((0, 8),), -0.2, 0.2)), 1000.0, 100000.0),
    }


def longitude_tables(orders, points):
    order_ids = jnp.arange(orders, dtype=jnp.int32)
    point_ids = jnp.arange(points, dtype=jnp.int32)
    phase = order_ids[:, None] * point_ids[None, :] % points
    angle = phase.astype(jnp.float32) * (2.0 * math.pi / points)
    cosine = jnp.cos(angle)
    sine_part = jnp.sin(angle)
    paired = jnp.stack([cosine, -sine_part], axis=1)
    synth_table = (paired / math.sqrt(orders)).astype(jnp.bfloat16)
    analysis_table = (paired * math.sqrt(2.0 / points)).astype(jnp.bfloat16)
    return (synth_table, analysis_table)

def rounded(values):
    return lax.optimization_barrier(values.astype(jnp.bfloat16)).astype(jnp.float32)

def tridiagonal_solve(right_side, diffusivity):
    degree = jnp.arange(ORDERS, dtype=jnp.float32)[:, None] + jnp.arange(DEG, dtype=jnp.float32)[None, :]
    angular = degree * (degree + 1.0)
    shell_ids = jnp.arange(NR, dtype=jnp.int32)

    def forward(carry, inputs):
        ratio_prev, value_prev = carry
        kappa_shell, source, shell_index = inputs
        lower = jnp.where(shell_index > 0, -kappa_shell, 0.0)
        upper = jnp.where(shell_index < NR - 1, -kappa_shell, 0.0)
        radius = (ROFF + shell_index).astype(jnp.float32)
        diagonal = 1.0 + 2.0 * kappa_shell + kappa_shell * angular / (radius * radius)
        pivot = diagonal - lower * ratio_prev
        ratio_now = upper / pivot
        value_now = (source - lower * value_prev) / pivot[:, None, :]
        return ((ratio_now, value_now), (ratio_now, value_now))
    blank_ratio = jnp.zeros((ORDERS, DEG), jnp.float32)
    blank_value = jnp.zeros((ORDERS, 2, DEG), jnp.float32)
    _, (ratios, values) = lax.scan(forward, (blank_ratio, blank_value), (diffusivity, right_side, shell_ids))

    def backward(beyond, inputs):
        ratio_now, value_now = inputs
        solved = value_now - ratio_now[:, None, :] * beyond
        return (solved, solved)
    _, solution = lax.scan(backward, blank_value, (ratios, values), reverse=True)
    return solution

def reference(scalar_field, radial_flow, legendre, diffusivity):
    synth_table, analysis_table = longitude_tables(ORDERS, NLON)
    synth_wide = synth_table.astype(jnp.float32)
    analysis_wide = analysis_table.astype(jnp.float32)
    legendre_wide = legendre.astype(jnp.float32)

    def shell_forcing(shell_pair):
        field_shell, flow_shell = shell_pair
        field_lat = rounded(jnp.einsum('mcj,mjt->mct', rounded(field_shell), legendre_wide))
        flow_lat = rounded(jnp.einsum('mcj,mjt->mct', rounded(flow_shell), legendre_wide))
        field_grid = jnp.einsum('mct,mcp->tp', field_lat, synth_wide)
        flow_grid = jnp.einsum('mct,mcp->tp', flow_lat, synth_wide)
        product = rounded(field_grid * flow_grid)
        product_modes = rounded(jnp.einsum('tp,mcp->mct', product, analysis_wide))
        return jnp.einsum('mct,mjt->mcj', product_modes, legendre_wide)
    forcing = lax.map(shell_forcing, (scalar_field, radial_flow))
    right_side = scalar_field + forcing
    return tridiagonal_solve(right_side, diffusivity)
```

```python
import functools
import math

import jax
import jax.numpy as jnp
import numpy as np
from jax import lax
from jax.experimental import pallas as pl
from jax.experimental.pallas import tpu as pltpu
from jax.sharding import PartitionSpec as P

NLON = 1536
VMEM_LIMIT = 56 * 1024 * 1024


def params(**more):
    return pltpu.CompilerParams(vmem_limit_bytes=VMEM_LIMIT, **more)


def grid_points(orders):
    needed = 3 * (orders - 1) + 1
    return next(q for q in range(128, NLON + 1, 128) if q >= needed and NLON % q == 0)


def longitude_tables(orders):
    points = grid_points(orders)
    stride = NLON // points
    phase = np.arange(orders)[:, None] * (np.arange(points) * stride)[None, :] % NLON
    angle = phase.astype(np.float32) * np.float32(2.0 * math.pi / NLON)
    paired = np.stack([np.cos(angle), -np.sin(angle)], axis=1).reshape(2 * orders, points)
    synth = (paired / np.float32(math.sqrt(orders))).astype(jnp.bfloat16)
    analysis = (paired * np.float32(math.sqrt(2.0 / NLON))).astype(jnp.bfloat16)
    return jnp.asarray(synth.T), jnp.asarray(analysis), float(stride)


def partner(here, hop, size):
    place, bit = 0, 1
    while bit < size:
        place = place + (here // bit + hop // bit) % 2 * bit
        bit *= 2
    return place


def whole_step(
    chunks, scale, kappa_ref, table_hbm, field_hbm, flow_hbm, synth_ref, analysis_ref, out_ref,
    field_ref, flow_ref, table_ref, spectral_ref, rows_ref, send_ref, recv_ref, back_send_ref, back_recv_ref,
    wide_ref, sum_ref, right_ref, alpha_ref, beta_ref, gamma_ref, ratio_ref, inverse_ref,
    slope_ref, slopes_ref, chain_ref, edge_ref, edges_ref,
    field_sem, table_sem, send_sem, recv_sem, back_send_sem, back_recv_sem, slope_send_sem, slope_recv_sem,
    edge_send_sem, edge_recv_sem,
):
    shells, ord_dev, _, degrees = field_ref.shape
    parts, rings = lax.axis_size("mode"), lax.axis_size("radial")
    me, ring = lax.axis_index("mode"), lax.axis_index("radial")
    mine = shells // parts
    count = 4 * shells
    width = 128
    blocks = degrees // 128
    nr_total = shells * rings
    halves, wide_rows = send_ref.shape[2], send_ref.shape[5]
    orders_half = ord_dev // halves
    groups = back_send_ref.shape[0]
    per = ord_dev // groups
    rows = 2 * per
    last = groups - 1
    steps = mine // 2
    pieces = [[(c, c + 1) for c in range(chunks)]]
    pieces += [[(0, chunks)] for _ in range(1, last)]
    pieces += [[(0, chunks - 2), (chunks - 2, chunks - 1), (chunks - 1, chunks)]]

    def field_copy(which, f):
        source, target = ((field_hbm, field_ref), (flow_hbm, flow_ref))[which]
        span = pl.ds(f * orders_half, orders_half)
        return pltpu.make_async_copy(source.at[:, span], target.at[:, span], field_sem.at[which, f])

    def first_table(f):
        span = pl.ds(f * orders_half, orders_half)
        return pltpu.make_async_copy(
            table_hbm.at[span, :, pl.ds(0, width)], table_ref.at[0, span], table_sem.at[f]
        )

    def table_copy(chunk):
        return pltpu.make_async_copy(
            table_hbm.at[:, :, pl.ds(chunk * width, width)], table_ref.at[chunk],
            table_sem.at[halves + chunk - 1],
        )

    for f in range(halves):
        field_copy(0, f).start()
        field_copy(1, f).start()
        first_table(f).start()

    barrier = pltpu.get_barrier_semaphore()
    for hop in range(1, parts):
        pl.semaphore_signal(
            barrier, inc=1, device_id={"mode": lax.rem(me + hop, parts)},
            device_id_type=pl.DeviceIdType.MESH,
        )
    for hop in range(1, rings):
        pl.semaphore_signal(
            barrier, inc=1, device_id={"radial": lax.rem(ring + hop, rings)},
            device_id_type=pl.DeviceIdType.MESH,
        )
    for chunk in range(1, chunks):
        table_copy(chunk).start()

    def exchange(axis, to, source, target, send, receive):
        return pltpu.make_async_remote_copy(
            src_ref=source, dst_ref=target, send_sem=send, recv_sem=receive,
            device_id={axis: to}, device_id_type=pl.DeviceIdType.MESH,
        )

    def first_copy(f, hop, slot):
        to = lax.rem(me + hop, parts)
        return exchange(
            "mode", to, send_ref.at[0, to, f], recv_ref.at[0, slot, f],
            send_sem.at[f, hop - 1], recv_sem.at[f, hop - 1],
        )

    def lat_copy(chunk, hop, slot):
        to = lax.rem(me + hop, parts)
        at = halves + chunk - 1
        return exchange(
            "mode", to, send_ref.at[chunk, to], recv_ref.at[chunk, slot],
            send_sem.at[at, hop - 1], recv_sem.at[at, hop - 1],
        )

    def lat_copies(chunk, hop, slot):
        return [first_copy(f, hop, slot) for f in range(halves)] if chunk == 0 else [lat_copy(chunk, hop, slot)]

    def back_copy(group, piece, hop, slot):
        to = lax.rem(me + hop, parts)
        first, end = pieces[group][piece]
        at = sum(len(p) for p in pieces[:group]) + piece
        span = pl.ds(first, end - first)
        return exchange(
            "mode", to, back_send_ref.at[group, to, span], back_recv_ref.at[group, slot, span],
            back_send_sem.at[at, hop - 1], back_recv_sem.at[at, hop - 1],
        )

    def send_back(group, piece):
        for hop in range(1, parts):
            back_copy(group, piece, hop, me).start()

    def edge_copy(group, hop, slot):
        return exchange(
            "radial", partner(ring, hop, rings), edge_ref.at[group], edges_ref.at[group, slot],
            edge_send_sem.at[group, hop - 1], edge_recv_sem.at[group, hop - 1],
        )

    def slope_copy(hop, slot):
        return exchange(
            "radial", partner(ring, hop, rings), slope_ref, slopes_ref.at[slot],
            slope_send_sem.at[hop - 1], slope_recv_sem.at[hop - 1],
        )

    def stack(order, carry):
        spectral_ref[order] = jnp.concatenate(
            [ref[:, order, half, :] for half in range(2) for ref in (field_ref, flow_ref)], axis=0
        ).astype(jnp.bfloat16)
        return carry

    def transform_of(chunk):
        def transform(order, carry):
            base = pl.multiple_of(order * count, count)
            rows_ref[pl.ds(base, count), :] = jnp.dot(
                spectral_ref[order], table_ref[chunk, order], preferred_element_type=jnp.float32
            )
            return carry

        return transform

    def pack_of(chunk, f):
        def pack(row, carry):
            which, shell = row // shells, row % shells
            picked = rows_ref[pl.ds(row + f * orders_half * count, wide_rows, stride=2 * shells), :]
            send_ref[chunk, shell // mine, f, which, shell % mine] = picked.astype(jnp.bfloat16)
            return carry

        return pack

    for f in range(halves):
        field_copy(0, f).wait()
        field_copy(1, f).wait()
        low, high = f * orders_half, (f + 1) * orders_half
        lax.fori_loop(low, high, stack, 0, unroll=4)
        first_table(f).wait()
        lax.fori_loop(low, high, transform_of(0), 0, unroll=4)
        lax.fori_loop(0, 2 * shells, pack_of(0, f), 0, unroll=8)
        if f == 0:
            pl.semaphore_wait(barrier, parts + rings - 2)
        for hop in range(1, parts):
            first_copy(f, hop, me).start()
    recv_ref[0, me] = send_ref[0, me]
    for chunk in range(1, chunks):
        table_copy(chunk).wait()
        lax.fori_loop(0, ord_dev, transform_of(chunk), 0, unroll=4)
        for f in range(halves):
            lax.fori_loop(0, 2 * shells, pack_of(chunk, f), 0, unroll=8)
        recv_ref[chunk, me] = send_ref[chunk, me]
        for hop in range(1, parts):
            lat_copy(chunk, hop, me).start()

    offset = nr_total * 7 // 13
    cut = [slice(block * 128, (block + 1) * 128) for block in range(blocks)]
    tile = (rows, 128)
    tiles = [(group, block) for group in range(groups) for block in range(blocks)]
    blank = jnp.zeros(tile, jnp.float32)
    unity = jnp.ones(tile, jnp.float32)

    def angular(group, block):
        degree = (
            me * ord_dev
            + group * per
            + block * 128
            + lax.broadcasted_iota(jnp.int32, tile, 0) % per
            + lax.broadcasted_iota(jnp.int32, tile, 1)
        ).astype(jnp.float32)
        return degree * (degree + 1.0)

    angulars = [angular(group, block) for group, block in tiles]

    def factor(shell, carry):
        kappa = jnp.full(tile, kappa_ref[shell], jnp.float32)
        spot = jnp.full(tile, ring * shells + shell, jnp.int32)
        lower = jnp.where(spot > 0, -kappa, 0.0)
        upper = jnp.where(spot < nr_total - 1, -kappa, 0.0)
        radius = (offset + spot).astype(jnp.float32)
        weight = kappa / (radius * radius)
        new = []
        for k, (group, block) in enumerate(tiles):
            ratio, pull = carry[k]
            diagonal = 1.0 + 2.0 * kappa + weight * angulars[k]
            inverse = 1.0 / (diagonal - lower * ratio)
            ratio = upper * inverse
            pull = -lower * pull * inverse
            inverse_ref[group, shell, :, cut[block]] = inverse
            ratio_ref[group, shell, :, cut[block]] = ratio
            beta_ref[group, shell, :, cut[block]] = pull
            new.append((ratio, pull))
        return tuple(new)

    outset = tuple((blank, unity) for _ in tiles)
    lax.fori_loop(0, shells, factor, outset)

    def unfactor(step, carry):
        shell = shells - 1 - step
        new = []
        for k, (group, block) in enumerate(tiles):
            beta, gamma = carry[k]
            ratio = ratio_ref[group, shell, :, cut[block]]
            beta = beta_ref[group, shell, :, cut[block]] - ratio * beta
            gamma = -ratio * gamma
            beta_ref[group, shell, :, cut[block]] = beta
            gamma_ref[group, shell, :, cut[block]] = gamma
            new.append((beta, gamma))
        return tuple(new)

    lax.fori_loop(0, shells, unfactor, outset)
    for group in range(groups):
        for side, shell in enumerate((0, shells - 1)):
            slope_ref[2 * side, group * per : (group + 1) * per] = beta_ref[group, shell, :per]
            slope_ref[2 * side + 1, group * per : (group + 1) * per] = gamma_ref[group, shell, :per]
    slopes_ref[ring] = slope_ref[...]
    for hop in range(1, rings):
        slope_copy(hop, ring).start()

    for chunk in range(chunks):
        for hop in range(1, parts):
            for copy in lat_copies(chunk, hop, lax.rem(me + parts - hop, parts)):
                copy.wait_recv()

        def multiply(step, carry):
            locals_ = [step * 2, step * 2 + 1]
            grids = []
            for which in range(2):
                lat = jnp.concatenate(
                    [
                        jnp.concatenate(
                            [
                                recv_ref[chunk, part, f, which, local]
                                for part in range(parts)
                                for f in range(halves)
                            ],
                            axis=0,
                        )
                        for local in locals_
                    ],
                    axis=1,
                )
                grids.append(jnp.dot(synth_ref[...], lat, preferred_element_type=jnp.float32))
            product = (grids[0] * grids[1]).astype(jnp.bfloat16)
            back = jnp.dot(analysis_ref[...], product, preferred_element_type=jnp.float32) * scale
            for part in range(parts):
                for group in range(groups):
                    base = (part * groups + group) * rows
                    back_send_ref[group, part, chunk, step] = jnp.concatenate(
                        [back[base : base + rows, k * width : (k + 1) * width] for k in range(2)], axis=0
                    ).astype(jnp.bfloat16)
            return carry

        lax.fori_loop(0, steps, multiply, 0, unroll=2)
        send_back(0, chunk)
    for group in range(1, groups):
        for piece in range(len(pieces[group])):
            send_back(group, piece)
    for group in range(groups):
        back_recv_ref[group, me] = back_send_ref[group, me]

    for hop in range(1, rings):
        slope_copy(hop, partner(ring, hop, rings)).wait_recv()
    for group, block in tiles:
        slope = blank
        for device in range(rings):
            head0, head1, tail0, tail1 = [
                jnp.concatenate([slopes_ref[device, k, group * per : (group + 1) * per, cut[block]]] * 2, axis=0)
                for k in range(4)
            ]
            inverse = 1.0 / (1.0 - head0 * slope)
            gain = head1 * inverse
            carried = tail0 * slope * inverse
            for k, value in enumerate((inverse, head0 * inverse, gain, carried, tail0 + carried * head0, slope)):
                chain_ref[group, device, k, :, cut[block]] = value
            slope = tail1 + tail0 * slope * gain

    def widen(group, first, end):
        for chunk in range(first, end):
            for part in range(parts):
                for step in range(steps):
                    base = (part * mine + 2 * step) * rows
                    wide_ref[chunk, base : base + 2 * rows, :] = back_recv_ref[
                        group, part, chunk, step
                    ].astype(jnp.float32)

    def untransform(group, first, end, final):
        for local in range(per):
            order = group * per + local
            picked = jnp.concatenate(
                [
                    jnp.concatenate(
                        [
                            wide_ref[chunk, pl.ds(2 * local + half, shells, stride=rows), :].astype(jnp.bfloat16)
                            for chunk in range(first, end)
                        ],
                        axis=1,
                    )
                    for half in range(2)
                ],
                axis=0,
            )
            table = jnp.concatenate([table_ref[chunk, order] for chunk in range(first, end)], axis=1)
            forcing = lax.dot_general(
                picked, table, (((1,), (1,)), ((), ())), preferred_element_type=jnp.float32
            )
            if first > 0:
                forcing = sum_ref[local] + forcing
            if not final:
                sum_ref[local] = forcing
                continue
            for half in range(2):
                right = field_ref[:, order, half, :] + forcing[half * shells : (half + 1) * shells]
                for block in range(blocks):
                    right_ref[block, pl.ds(half * per + local, shells, stride=rows), :] = right[:, cut[block]]

    empty = tuple(blank for _ in range(blocks))

    def solve(group):
        def forward(shell, carry):
            index = ring * shells + shell
            lower = jnp.where(jnp.full(tile, index, jnp.int32) > 0, -kappa_ref[shell], 0.0)
            start = pl.multiple_of(shell * rows, rows)
            new = []
            for block in range(blocks):
                value = (right_ref[block, pl.ds(start, rows), :] - lower * carry[block]) * inverse_ref[
                    group, shell, :, cut[block]
                ]
                alpha_ref[group, shell, :, cut[block]] = value
                new.append(value)
            return tuple(new)

        lax.fori_loop(0, shells, forward, empty, unroll=4)

        def backward(step, carry):
            shell = shells - 1 - step
            new = []
            for block in range(blocks):
                value = (
                    alpha_ref[group, shell, :, cut[block]]
                    - ratio_ref[group, shell, :, cut[block]] * carry[block]
                )
                alpha_ref[group, shell, :, cut[block]] = value
                new.append(value)
            return tuple(new)

        lax.fori_loop(0, shells, backward, empty, unroll=4)
        for side, shell in enumerate((0, shells - 1)):
            edge_ref[group, side] = alpha_ref[group, shell]
        for hop in reversed(range(1, rings)):
            edge_copy(group, hop, ring).start()
        edges_ref[group, ring] = edge_ref[group]

    def finish(group):
        for hop in reversed(range(1, rings)):
            edge_copy(group, hop, partner(ring, hop, rings)).wait_recv()
        spot = jnp.full(tile, ring, jnp.int32)
        befores, afters = [], []
        for block in range(blocks):
            known, consts, left, tilt = blank, [], blank, blank
            for device in range(rings):
                first, end = [edges_ref[group, device, side, :, cut[block]] for side in range(2)]
                inverse, headed, gain, carried, through, slope = [
                    chain_ref[group, device, k, :, cut[block]] for k in range(6)
                ]
                here = spot == device
                left = jnp.where(here, known, left)
                tilt = jnp.where(here, slope, tilt)
                consts.append(inverse * first + headed * known)
                known = end + carried * first + through * known
            beyond, before, after = blank, blank, blank
            for device in reversed(range(rings)):
                here = spot == device
                start = consts[device] + chain_ref[group, device, 2, :, cut[block]] * beyond
                before = jnp.where(here, left + tilt * start, before)
                after = jnp.where(here, beyond, after)
                beyond = start
            befores.append(before)
            afters.append(after)

        def emit(shell, carry):
            for block in range(blocks):
                value = (
                    alpha_ref[group, shell, :, cut[block]]
                    + beta_ref[group, shell, :, cut[block]] * befores[block]
                    + gamma_ref[group, shell, :, cut[block]] * afters[block]
                )
                for half in range(2):
                    out_ref[shell, group * per : (group + 1) * per, half, cut[block]] = value[
                        half * per : (half + 1) * per
                    ]
            return carry

        lax.fori_loop(0, shells, emit, 0, unroll=4)

    for group in range(groups):
        for piece, (first, end) in enumerate(pieces[group]):
            for hop in range(1, parts):
                back_copy(group, piece, hop, lax.rem(me + parts - hop, parts)).wait_recv()
            if group == last:
                widen(group, first, end)
                untransform(group, first, end, end == chunks)
        if group < last:
            widen(group, 0, chunks)
            untransform(group, 0, chunks, True)
        solve(group)
        if group == 0:
            for hop in range(1, parts):
                for chunk in range(chunks):
                    for copy in lat_copies(chunk, hop, me):
                        copy.wait_send()
            for hop in range(1, rings):
                slope_copy(hop, ring).wait_send()
        else:
            finish(group - 1)
            for piece in range(len(pieces[group - 1])):
                for hop in range(1, parts):
                    back_copy(group - 1, piece, hop, me).wait_send()
            for hop in range(1, rings):
                edge_copy(group - 1, hop, ring).wait_send()
    for piece in range(len(pieces[last])):
        for hop in range(1, parts):
            back_copy(last, piece, hop, me).wait_send()
    finish(last)
    for hop in range(1, rings):
        edge_copy(last, hop, ring).wait_send()


def on_device(scalar_field, radial_flow, legendre, diffusivity):
    shells, ord_dev, _, degrees = scalar_field.shape
    lats = legendre.shape[2]
    parts, rings = lax.axis_size("mode"), lax.axis_size("radial")
    mine = shells // parts
    synth, analysis, scale = longitude_tables(ord_dev * parts)
    width, per, orders_half = 128, 4, 8
    chunks, blocks = lats // width, degrees // 128
    halves, groups = ord_dev // orders_half, ord_dev // per
    assert rings & (rings - 1) == 0 and mine % 2 == 0
    assert lats % width == 0 and degrees % 128 == 0 and ord_dev % orders_half == 0
    back_pieces = chunks + (groups - 2) + 3
    bf16, f32 = jnp.bfloat16, jnp.float32
    vmem, hbm = pl.BlockSpec(memory_space=pltpu.VMEM), pl.BlockSpec(memory_space=pltpu.HBM)
    dma = pltpu.SemaphoreType.DMA
    solved = pltpu.VMEM((groups, shells, 2 * per, degrees), f32)
    return pl.pallas_call(
        functools.partial(whole_step, chunks, scale),
        in_specs=[pl.BlockSpec(memory_space=pltpu.SMEM), hbm, hbm, hbm, vmem, vmem],
        out_specs=vmem,
        out_shape=pltpu.VMEM(scalar_field.shape, f32),
        scratch_shapes=[
            pltpu.VMEM(scalar_field.shape, f32),
            pltpu.VMEM(scalar_field.shape, f32),
            pltpu.VMEM((chunks, ord_dev, degrees, width), bf16),
            pltpu.VMEM((ord_dev, 4 * shells, degrees), bf16),
            pltpu.VMEM((4 * shells * ord_dev, width), f32),
            pltpu.VMEM((chunks, parts, halves, 2, mine, 2 * orders_half, width), bf16),
            pltpu.VMEM((chunks, parts, halves, 2, mine, 2 * orders_half, width), bf16),
            pltpu.VMEM((groups, parts, chunks, mine // 2, 4 * per, width), bf16),
            pltpu.VMEM((groups, parts, chunks, mine // 2, 4 * per, width), bf16),
            pltpu.VMEM((chunks, shells * 2 * per, width), f32),
            pltpu.VMEM((per, 2 * shells, degrees), f32),
            pltpu.VMEM((blocks, shells * 2 * per, 128), f32),
            solved, solved, solved, solved, solved,
            pltpu.VMEM((4, ord_dev, degrees), f32),
            pltpu.VMEM((rings, 4, ord_dev, degrees), f32),
            pltpu.VMEM((groups, rings, 6, 2 * per, degrees), f32),
            pltpu.VMEM((groups, 2, 2 * per, degrees), f32),
            pltpu.VMEM((groups, rings, 2, 2 * per, degrees), f32),
            dma((2, halves)),
            dma((halves + chunks - 1,)),
            dma((halves + chunks - 1, parts - 1)),
            dma((halves + chunks - 1, parts - 1)),
            dma((back_pieces, parts - 1)),
            dma((back_pieces, parts - 1)),
            dma((rings - 1,)),
            dma((rings - 1,)),
            dma((groups, rings - 1)),
            dma((groups, rings - 1)),
        ],
        compiler_params=params(collective_id=0, has_side_effects=True),
        name="whole_step",
    )(diffusivity, legendre, scalar_field, radial_flow, synth, analysis)


def solution(mesh):
    return jax.shard_map(
        on_device,
        mesh=mesh,
        in_specs=(
            P("radial", "mode", None, None),
            P("radial", "mode", None, None),
            P("mode", None, None),
            P("radial"),
        ),
        out_specs=P("radial", "mode", None, None),
        check_vma=False,
    )
```

```python
import functools
import math

import jax
import jax.numpy as jnp
import numpy as np
from jax import lax
from jax.experimental import pallas as pl
from jax.experimental.pallas import tpu as pltpu
from jax.sharding import PartitionSpec as P

NLON = 1536
VMEM_LIMIT = 56 * 1024 * 1024


def params(**more):
    return pltpu.CompilerParams(vmem_limit_bytes=VMEM_LIMIT, **more)


def grid_points(orders):
    needed = 3 * (orders - 1) + 1
    return next(q for q in range(128, NLON + 1, 128) if q >= needed and NLON % q == 0)


def longitude_tables(orders):
    points = grid_points(orders)
    stride = NLON // points
    phase = np.arange(orders)[:, None] * (np.arange(points) * stride)[None, :] % NLON
    angle = phase.astype(np.float32) * np.float32(2.0 * math.pi / NLON)
    paired = np.stack([np.cos(angle), -np.sin(angle)], axis=1).reshape(2 * orders, points)
    synth = (paired / np.float32(math.sqrt(orders))).astype(jnp.bfloat16)
    analysis = (paired * np.float32(math.sqrt(2.0 / NLON))).astype(jnp.bfloat16)
    return jnp.asarray(synth.T), jnp.asarray(analysis), float(stride)


def partner(here, hop, size):
    place, bit = 0, 1
    while bit < size:
        place = place + (here // bit + hop // bit) % 2 * bit
        bit *= 2
    return place


def whole_step(
    scale, kappa_hbm, table_hbm, field_hbm, flow_hbm, synth_hbm, analysis_hbm, out_ref,
    kappa_ref, synth_ref, analysis_ref, field_ref, flow_ref, table_ref, spectral_ref, rows_ref,
    send_ref, recv_ref, back_send_ref, back_recv_ref,
    wide_ref, sum_ref, right_ref, alpha_ref, beta_ref, gamma_ref, ratio_ref, inverse_ref,
    slope_ref, slopes_ref, chain_ref, edge_ref, edges_ref, half_edge_ref, half_edges_ref,
    small_sem, field_sem, table_sem, send_sem, recv_sem, back_send_sem, back_recv_sem,
    slope_send_sem, slope_recv_sem, edge_send_sem, edge_recv_sem,
):
    shells, ord_dev, _, degrees = field_ref.shape
    parts, rings = lax.axis_size("mode"), lax.axis_size("radial")
    me, ring = lax.axis_index("mode"), lax.axis_index("radial")
    mine = shells // parts
    count = 4 * shells
    width = 128
    blocks = degrees // 128
    nr_total = shells * rings
    chunks, halves, wide_rows = send_ref.shape[1], send_ref.shape[2], send_ref.shape[5]
    orders_half = ord_dev // halves
    groups = back_send_ref.shape[0]
    per = ord_dev // groups
    rows = 2 * per
    pairs, full = groups // 2, 2 * rows
    units = [((2 * pair, 2 * pair + 1), pair, 0, full) for pair in range(pairs - 1)]
    units += [((groups - 2 + k,), pairs - 1, k * rows, (k + 1) * rows) for k in range(2)]
    last = len(units) - 1
    out_pieces = [(1, 2), (2, chunks - 2), (chunks - 2, chunks - 1), (chunks - 1, chunks)]
    early = 2
    pieces = [[(0, chunks - 1), (chunks - 1, chunks)] for _ in range(early)]
    pieces += [[(0, chunks)] for _ in range(early, groups - 1)]
    pieces += [[(0, chunks - 1), (chunks - 1, chunks)]]

    def field_copy(which, f):
        source, target = ((field_hbm, field_ref), (flow_hbm, flow_ref))[which]
        span = pl.ds(f * orders_half, orders_half)
        return pltpu.make_async_copy(source.at[:, span], target.at[:, span], field_sem.at[which, f])

    def first_table(f):
        span = pl.ds(f * orders_half, orders_half)
        return pltpu.make_async_copy(
            table_hbm.at[span, :, pl.ds(0, width)], table_ref.at[0, span], table_sem.at[f]
        )

    def table_copy(chunk):
        return pltpu.make_async_copy(
            table_hbm.at[:, :, pl.ds(chunk * width, width)], table_ref.at[chunk],
            table_sem.at[halves + chunk - 1],
        )

    small = [
        pltpu.make_async_copy(source, target, small_sem.at[k])
        for k, (source, target) in enumerate(
            ((kappa_hbm, kappa_ref), (synth_hbm, synth_ref), (analysis_hbm, analysis_ref))
        )
    ]

    def load_half(f):
        field_copy(0, f).start()
        field_copy(1, f).start()
        first_table(f).start()

    load_half(0)
    barrier = pltpu.get_barrier_semaphore()
    for hop in range(1, parts):
        pl.semaphore_signal(
            barrier, inc=1, device_id={"mode": lax.rem(me + hop, parts)},
            device_id_type=pl.DeviceIdType.MESH,
        )
    for hop in range(1, rings):
        pl.semaphore_signal(
            barrier, inc=1, device_id={"radial": lax.rem(ring + hop, rings)},
            device_id_type=pl.DeviceIdType.MESH,
        )
    for f in range(1, halves):
        load_half(f)
    for chunk in range(1, chunks):
        table_copy(chunk).start()
    for copy in small:
        copy.start()

    def exchange(axis, to, source, target, send, receive):
        return pltpu.make_async_remote_copy(
            src_ref=source, dst_ref=target, send_sem=send, recv_sem=receive,
            device_id={axis: to}, device_id_type=pl.DeviceIdType.MESH,
        )

    def first_copy(f, hop, slot):
        to = lax.rem(me + hop, parts)
        return exchange(
            "mode", to, send_ref.at[to, 0, f], recv_ref.at[slot, 0, f],
            send_sem.at[f, hop - 1], recv_sem.at[f, hop - 1],
        )

    def lat_copy(piece, hop, slot):
        to = lax.rem(me + hop, parts)
        first, end = out_pieces[piece]
        span = pl.ds(first, end - first)
        at = halves + piece
        return exchange(
            "mode", to, send_ref.at[to, span], recv_ref.at[slot, span],
            send_sem.at[at, hop - 1], recv_sem.at[at, hop - 1],
        )

    def lat_copies(piece, hop, slot):
        return [first_copy(f, hop, slot) for f in range(halves)] if piece < 0 else [lat_copy(piece, hop, slot)]

    def back_copy(group, piece, hop, slot):
        to = lax.rem(me + hop, parts)
        first, end = pieces[group][piece]
        at = sum(len(p) for p in pieces[:group]) + piece
        span = pl.ds(first, end - first)
        return exchange(
            "mode", to, back_send_ref.at[group, to, span], back_recv_ref.at[group, slot, span],
            back_send_sem.at[at, hop - 1], back_recv_sem.at[at, hop - 1],
        )

    def send_back(group, piece):
        for hop in range(1, parts):
            back_copy(group, piece, hop, me).start()

    def edge_buffers(unit):
        return (edge_ref.at[unit], edges_ref.at[unit]) if unit < pairs - 1 else (
            half_edge_ref.at[unit - pairs + 1], half_edges_ref.at[unit - pairs + 1]
        )

    def edge_copy(unit, hop, slot):
        here, there = edge_buffers(unit)
        return exchange(
            "radial", partner(ring, hop, rings), here, there.at[slot],
            edge_send_sem.at[unit, hop - 1], edge_recv_sem.at[unit, hop - 1],
        )

    def slope_copy(hop, slot):
        return exchange(
            "radial", partner(ring, hop, rings), slope_ref, slopes_ref.at[slot],
            slope_send_sem.at[hop - 1], slope_recv_sem.at[hop - 1],
        )

    def stack(order, carry):
        spectral_ref[order] = jnp.concatenate(
            [ref[:, order, half, :] for half in range(2) for ref in (field_ref, flow_ref)], axis=0
        ).astype(jnp.bfloat16)
        return carry

    def transform_of(chunk):
        def transform(order, carry):
            base = pl.multiple_of(order * count, count)
            rows_ref[pl.ds(base, count), :] = jnp.dot(
                spectral_ref[order], table_ref[chunk, order], preferred_element_type=jnp.float32
            )
            return carry

        return transform

    def picked(row, f):
        values = rows_ref[pl.ds(row + f * orders_half * count, wide_rows, stride=2 * shells), :]
        return values.astype(jnp.bfloat16)

    def pack_of(chunk, f):
        def pack(row, carry):
            which, shell = row // shells, row % shells
            send_ref[shell // mine, chunk, f, which, shell % mine] = picked(row, f)
            return carry

        return pack

    def pack_for(to, target, f):
        def pack(row, carry):
            which, local = row // mine, row % mine
            target[to, 0, f, which, local] = picked(which * shells + to * mine + local, f)
            return carry

        lax.fori_loop(0, 2 * mine, pack, 0, unroll=8)

    for f in range(halves):
        field_copy(0, f).wait()
        field_copy(1, f).wait()
        low, high = f * orders_half, (f + 1) * orders_half
        lax.fori_loop(low, high, stack, 0, unroll=4)
        first_table(f).wait()
        lax.fori_loop(low, high, transform_of(0), 0, unroll=4)
        for hop in range(1, parts):
            pack_for(lax.rem(me + hop, parts), send_ref, f)
            if f == 0 and hop == 1:
                pl.semaphore_wait(barrier, parts + rings - 2)
            first_copy(f, hop, me).start()
        pack_for(me, recv_ref, f)
    for piece, (first, end) in enumerate(out_pieces):
        for chunk in range(first, end):
            table_copy(chunk).wait()
            lax.fori_loop(0, ord_dev, transform_of(chunk), 0, unroll=4)
            for f in range(halves):
                lax.fori_loop(0, 2 * shells, pack_of(chunk, f), 0, unroll=8)
            recv_ref[me, chunk] = send_ref[me, chunk]
        for hop in range(1, parts):
            lat_copy(piece, hop, me).start()

    for copy in small:
        copy.wait()
    offset = nr_total * 7 // 13
    cut = [slice(block * 128, (block + 1) * 128) for block in range(blocks)]
    tile = (full, 128)
    tiles = [(pair, block) for pair in range(pairs) for block in range(blocks)]
    blank = jnp.zeros(tile, jnp.float32)
    unity = jnp.ones(tile, jnp.float32)

    def angular(pair, block):
        degree = (
            me * ord_dev
            + pair * 2 * per
            + block * 128
            + lax.broadcasted_iota(jnp.int32, tile, 0) // 2
            + lax.broadcasted_iota(jnp.int32, tile, 1)
        ).astype(jnp.float32)
        return degree * (degree + 1.0)

    angulars = [angular(pair, block) for pair, block in tiles]

    def factor(shell, carry):
        kappa = jnp.full(tile, kappa_ref[shell], jnp.float32)
        spot = jnp.full(tile, ring * shells + shell, jnp.int32)
        lower = jnp.where(spot > 0, -kappa, 0.0)
        upper = jnp.where(spot < nr_total - 1, -kappa, 0.0)
        radius = (offset + spot).astype(jnp.float32)
        weight = kappa / (radius * radius)
        new = []
        for k, (pair, block) in enumerate(tiles):
            ratio, pull = carry[k]
            diagonal = 1.0 + 2.0 * kappa + weight * angulars[k]
            inverse = 1.0 / (diagonal - lower * ratio)
            ratio = upper * inverse
            pull = -lower * pull * inverse
            inverse_ref[pair, shell, :, cut[block]] = inverse
            ratio_ref[pair, shell, :, cut[block]] = ratio
            beta_ref[pair, shell, :, cut[block]] = pull
            new.append((ratio, pull))
        return tuple(new)

    outset = tuple((blank, unity) for _ in tiles)
    lax.fori_loop(0, shells, factor, outset)

    def unfactor(step, carry):
        shell = shells - 1 - step
        new = []
        for k, (pair, block) in enumerate(tiles):
            beta, gamma = carry[k]
            ratio = ratio_ref[pair, shell, :, cut[block]]
            beta = beta_ref[pair, shell, :, cut[block]] - ratio * beta
            gamma = -ratio * gamma
            beta_ref[pair, shell, :, cut[block]] = beta
            gamma_ref[pair, shell, :, cut[block]] = gamma
            new.append((beta, gamma))
        return tuple(new)

    lax.fori_loop(0, shells, unfactor, outset)
    for pair in range(pairs):
        for side, shell in enumerate((0, shells - 1)):
            slope_ref[2 * side, pair] = beta_ref[pair, shell]
            slope_ref[2 * side + 1, pair] = gamma_ref[pair, shell]
    slopes_ref[ring] = slope_ref[...]
    for hop in range(1, rings):
        slope_copy(hop, ring).start()

    def multiply_of(chunk):
        def back_of(locals_):
            grids = []
            for which in range(2):
                lat = jnp.concatenate(
                    [
                        jnp.concatenate(
                            [
                                recv_ref[part, chunk, f, which, local]
                                for part in range(parts)
                                for f in range(halves)
                            ],
                            axis=0,
                        )
                        for local in locals_
                    ],
                    axis=1,
                )
                grids.append(jnp.dot(synth_ref[...], lat, preferred_element_type=jnp.float32))
            product = (grids[0] * grids[1]).astype(jnp.bfloat16)
            return jnp.dot(analysis_ref[...], product, preferred_element_type=jnp.float32) * scale

        def multiply(step, carry):
            backs = [back_of((step * 4 + 2 * k, step * 4 + 2 * k + 1)) for k in range(2)]
            for part in range(parts):
                for group in range(groups):
                    base = (part * groups + group) * rows
                    back_send_ref[group, part, chunk, step] = jnp.concatenate(
                        [back[base : base + rows, k * width : (k + 1) * width] for back in backs for k in range(2)],
                        axis=0,
                    ).astype(jnp.bfloat16)
            return carry

        return multiply

    for piece in range(-1, len(out_pieces)):
        for hop in range(1, parts):
            for copy in lat_copies(piece, hop, lax.rem(me + parts - hop, parts)):
                copy.wait_recv()
        first, end = (0, 1) if piece < 0 else out_pieces[piece]
        for chunk in range(first, end):
            lax.fori_loop(0, mine // 4, multiply_of(chunk), 0)
        if end >= chunks - 1:
            for group in range(early):
                send_back(group, end - chunks + 1)
    for group in range(early, groups):
        for piece in range(len(pieces[group])):
            send_back(group, piece)
    for group in range(groups):
        back_recv_ref[group, me] = back_send_ref[group, me]

    for hop in range(1, rings):
        slope_copy(hop, partner(ring, hop, rings)).wait_recv()
    for pair, block in tiles:
        slope = blank
        for device in range(rings):
            head0, head1, tail0, tail1 = [slopes_ref[device, k, pair, :, cut[block]] for k in range(4)]
            inverse = 1.0 / (1.0 - head0 * slope)
            gain = head1 * inverse
            carried = tail0 * slope * inverse
            for k, value in enumerate((inverse, head0 * inverse, gain, carried, tail0 + carried * head0, slope)):
                chain_ref[pair, device, k, :, cut[block]] = value
            slope = tail1 + tail0 * slope * gain

    def widen(group, first, end):
        for chunk in range(first, end):
            for part in range(parts):
                for step in range(mine // 4):
                    base = (part * mine + 4 * step) * rows
                    wide_ref[chunk, base : base + 4 * rows, :] = back_recv_ref[
                        group, part, chunk, step
                    ].astype(jnp.float32)

    def untransform(group, first, end):
        for local in range(per):
            order = group * per + local
            stacked = jnp.concatenate(
                [
                    jnp.concatenate(
                        [
                            wide_ref[chunk, pl.ds(2 * local + half, shells, stride=rows), :].astype(jnp.bfloat16)
                            for chunk in range(first, end)
                        ],
                        axis=1,
                    )
                    for half in range(2)
                ],
                axis=0,
            )
            table = jnp.concatenate([table_ref[chunk, order] for chunk in range(first, end)], axis=1)
            forcing = lax.dot_general(
                stacked, table, (((1,), (1,)), ((), ())), preferred_element_type=jnp.float32
            )
            if first > 0:
                forcing = sum_ref[local] + forcing
            if end < chunks:
                sum_ref[local] = forcing
                continue
            for half in range(2):
                right = field_ref[:, order, half, :] + forcing[half * shells : (half + 1) * shells]
                row = (group % 2) * rows + 2 * local + half
                for block in range(blocks):
                    right_ref[block, pl.ds(row, shells, stride=full), :] = right[:, cut[block]]

    def solve(unit):
        _, pair, low, high = units[unit]
        empty = tuple(jnp.zeros((high - low, 128), jnp.float32) for _ in range(blocks))

        def forward(shell, carry):
            index = ring * shells + shell
            lower = jnp.where(jnp.full(empty[0].shape, index, jnp.int32) > 0, -kappa_ref[shell], 0.0)
            start = shell * full
            new = []
            for block in range(blocks):
                right = right_ref[block, pl.ds(pl.multiple_of(start, full) + low, high - low), :]
                value = (right - lower * carry[block]) * inverse_ref[pair, shell, low:high, cut[block]]
                alpha_ref[pair, shell, low:high, cut[block]] = value
                new.append(value)
            return tuple(new)

        lax.fori_loop(0, shells, forward, empty, unroll=4)

        def backward(step, carry):
            shell = shells - 1 - step
            new = []
            for block in range(blocks):
                value = (
                    alpha_ref[pair, shell, low:high, cut[block]]
                    - ratio_ref[pair, shell, low:high, cut[block]] * carry[block]
                )
                alpha_ref[pair, shell, low:high, cut[block]] = value
                new.append(value)
            return tuple(new)

        lax.fori_loop(0, shells, backward, empty, unroll=4)
        here, there = edge_buffers(unit)
        for side, shell in enumerate((0, shells - 1)):
            here[side * (high - low) : (side + 1) * (high - low)] = alpha_ref[pair, shell, low:high]
        for hop in reversed(range(1, rings)):
            edge_copy(unit, hop, ring).start()
        there[ring] = here[...]

    def finish(unit):
        members, pair, low, high = units[unit]
        size = high - low
        for hop in reversed(range(1, rings)):
            edge_copy(unit, hop, partner(ring, hop, rings)).wait_recv()
        _, there = edge_buffers(unit)
        empty = jnp.zeros((size, 128), jnp.float32)
        spot = jnp.full((size, 128), ring, jnp.int32)
        befores, afters = [], []
        for block in range(blocks):
            known, consts, left, tilt = empty, [], empty, empty
            for device in range(rings):
                first, end = [there[device, side * size : (side + 1) * size, cut[block]] for side in range(2)]
                inverse, headed, _, carried, through, slope = [
                    chain_ref[pair, device, k, low:high, cut[block]] for k in range(6)
                ]
                here = spot == device
                left = jnp.where(here, known, left)
                tilt = jnp.where(here, slope, tilt)
                consts.append(inverse * first + headed * known)
                known = end + carried * first + through * known
            beyond, before, after = empty, empty, empty
            for device in reversed(range(rings)):
                here = spot == device
                start = consts[device] + chain_ref[pair, device, 2, low:high, cut[block]] * beyond
                before = jnp.where(here, left + tilt * start, before)
                after = jnp.where(here, beyond, after)
                beyond = start
            befores.append(before)
            afters.append(after)

        def emit(shell, carry):
            for block in range(blocks):
                value = (
                    alpha_ref[pair, shell, low:high, cut[block]]
                    + beta_ref[pair, shell, low:high, cut[block]] * befores[block]
                    + gamma_ref[pair, shell, low:high, cut[block]] * afters[block]
                )
                for k in range(size // 2):
                    out_ref[shell, members[0] * per + k, :, cut[block]] = value[2 * k : 2 * k + 2]
            return carry

        lax.fori_loop(0, shells, emit, 0, unroll=4)

    def settle(unit):
        for group in units[unit][0]:
            for piece in range(len(pieces[group])):
                for hop in range(1, parts):
                    back_copy(group, piece, hop, me).wait_send()

    for unit, (members, _, _, _) in enumerate(units):
        for group in members:
            for piece, (first, end) in enumerate(pieces[group]):
                for hop in range(1, parts):
                    back_copy(group, piece, hop, lax.rem(me + parts - hop, parts)).wait_recv()
                if unit == last:
                    widen(group, first, end)
                    untransform(group, first, end)
            if unit < last:
                widen(group, 0, chunks)
                untransform(group, 0, chunks)
        solve(unit)
        if unit == 0:
            for hop in range(1, parts):
                for piece in range(-1, len(out_pieces)):
                    for copy in lat_copies(piece, hop, me):
                        copy.wait_send()
            for hop in range(1, rings):
                slope_copy(hop, ring).wait_send()
        else:
            finish(unit - 1)
            settle(unit - 1)
            for hop in range(1, rings):
                edge_copy(unit - 1, hop, ring).wait_send()
    settle(last)
    finish(last)
    for hop in range(1, rings):
        edge_copy(last, hop, ring).wait_send()


def on_device(scalar_field, radial_flow, legendre, diffusivity):
    shells, ord_dev, _, degrees = scalar_field.shape
    lats = legendre.shape[2]
    parts, rings = lax.axis_size("mode"), lax.axis_size("radial")
    mine = shells // parts
    synth, analysis, scale = longitude_tables(ord_dev * parts)
    width, per, orders_half = 128, 2, 8
    chunks, blocks = lats // width, degrees // 128
    halves, groups = ord_dev // orders_half, ord_dev // per
    pairs, full = groups // 2, 4 * per
    assert rings & (rings - 1) == 0 and mine % 4 == 0 and chunks >= 5
    assert lats % width == 0 and degrees % 128 == 0 and ord_dev % orders_half == 0
    bf16, f32 = jnp.bfloat16, jnp.float32
    vmem, hbm = pl.BlockSpec(memory_space=pltpu.VMEM), pl.BlockSpec(memory_space=pltpu.HBM)
    dma = pltpu.SemaphoreType.DMA
    solved = pltpu.VMEM((pairs, shells, full, degrees), f32)
    there = pltpu.VMEM((parts, chunks, halves, 2, mine, 2 * orders_half, width), bf16)
    back = pltpu.VMEM((groups, parts, chunks, mine // 4, 8 * per, width), bf16)
    return pl.pallas_call(
        functools.partial(whole_step, scale),
        in_specs=[hbm] * 6,
        out_specs=vmem,
        out_shape=pltpu.VMEM(scalar_field.shape, f32),
        scratch_shapes=[
            pltpu.SMEM(diffusivity.shape, f32),
            pltpu.VMEM(synth.shape, bf16),
            pltpu.VMEM(analysis.shape, bf16),
            pltpu.VMEM(scalar_field.shape, f32),
            pltpu.VMEM(scalar_field.shape, f32),
            pltpu.VMEM((chunks, ord_dev, degrees, width), bf16),
            pltpu.VMEM((ord_dev, 4 * shells, degrees), bf16),
            pltpu.VMEM((4 * shells * ord_dev, width), f32),
            there, there, back, back,
            pltpu.VMEM((chunks, shells * 2 * per, width), f32),
            pltpu.VMEM((per, 2 * shells, degrees), f32),
            pltpu.VMEM((blocks, shells * full, 128), f32),
            solved, solved, solved, solved, solved,
            pltpu.VMEM((4, pairs, full, degrees), f32),
            pltpu.VMEM((rings, 4, pairs, full, degrees), f32),
            pltpu.VMEM((pairs, rings, 6, full, degrees), f32),
            pltpu.VMEM((pairs - 1, 2 * full, degrees), f32),
            pltpu.VMEM((pairs - 1, rings, 2 * full, degrees), f32),
            pltpu.VMEM((2, full, degrees), f32),
            pltpu.VMEM((2, rings, full, degrees), f32),
            dma((3,)),
            dma((2, halves)),
            dma((halves + chunks - 1,)),
            dma((halves + 4, parts - 1)),
            dma((halves + 4, parts - 1)),
            dma((groups + 3, parts - 1)),
            dma((groups + 3, parts - 1)),
            dma((rings - 1,)),
            dma((rings - 1,)),
            dma((pairs + 1, rings - 1)),
            dma((pairs + 1, rings - 1)),
        ],
        compiler_params=params(collective_id=0, has_side_effects=True),
        name="whole_step",
    )(diffusivity, legendre, scalar_field, radial_flow, synth, analysis)


def solution(mesh):
    return jax.shard_map(
        on_device,
        mesh=mesh,
        in_specs=(
            P("radial", "mode", None, None),
            P("radial", "mode", None, None),
            P("mode", None, None),
            P("radial"),
        ),
        out_specs=P("radial", "mode", None, None),
        check_vma=False,
    )
```

```python
import functools
import math

import jax
import jax.numpy as jnp
import numpy as np
from jax import lax
from jax.experimental import pallas as pl
from jax.experimental.pallas import tpu as pltpu
from jax.sharding import PartitionSpec as P

NLON = 1536
VMEM_LIMIT = 56 * 1024 * 1024


def params(**more):
    return pltpu.CompilerParams(vmem_limit_bytes=VMEM_LIMIT, **more)


def grid_points(orders):
    needed = 3 * (orders - 1) + 1
    return next(q for q in range(128, NLON + 1, 128) if q >= needed and NLON % q == 0)


def longitude_tables(orders):
    points = grid_points(orders)
    stride = NLON // points
    phase = np.arange(orders)[:, None] * (np.arange(points) * stride)[None, :] % NLON
    angle = phase.astype(np.float32) * np.float32(2.0 * math.pi / NLON)
    paired = np.stack([np.cos(angle), -np.sin(angle)], axis=1).reshape(2 * orders, points)
    synth = (paired / np.float32(math.sqrt(orders))).astype(jnp.bfloat16)
    analysis = (paired * np.float32(math.sqrt(2.0 / NLON))).astype(jnp.bfloat16)
    return jnp.asarray(synth.T), jnp.asarray(analysis), float(stride)


def partner(here, hop, size):
    place, bit = 0, 1
    while bit < size:
        place = place + (here // bit + hop // bit) % 2 * bit
        bit *= 2
    return place


def whole_step(
    scale, kappa_hbm, table_hbm, field_hbm, flow_hbm, synth_hbm, analysis_hbm, out_ref,
    kappa_ref, synth_ref, analysis_ref, field_ref, flow_ref, table_ref, spectral_ref, rows_ref,
    send_ref, recv_ref, back_send_ref, back_recv_ref,
    wide_ref, sum_ref, right_ref, alpha_ref, beta_ref, gamma_ref, ratio_ref, inverse_ref, first_ref, end_ref,
    slope_ref, slopes_ref, chain_ref, edge_ref, edges_ref, half_edge_ref, half_edges_ref,
    small_sem, field_sem, table_sem, send_sem, recv_sem, back_send_sem, back_recv_sem,
    slope_send_sem, slope_recv_sem, edge_send_sem, edge_recv_sem,
):
    shells, ord_dev, _, degrees = field_ref.shape
    parts, rings = lax.axis_size("mode"), lax.axis_size("radial")
    me, ring = lax.axis_index("mode"), lax.axis_index("radial")
    mine = shells // parts
    count = 4 * shells
    width = 128
    blocks = degrees // 128
    nr_total = shells * rings
    chunks, halves, wide_rows = send_ref.shape[1], send_ref.shape[2], send_ref.shape[5]
    orders_half = ord_dev // halves
    groups = back_send_ref.shape[0]
    per = ord_dev // groups
    rows = 2 * per
    pairs, full = groups // 2, 2 * rows
    units = [((2 * pair, 2 * pair + 1), pair, 0, full) for pair in range(pairs - 1)]
    units += [((groups - 2 + k,), pairs - 1, k * rows, (k + 1) * rows) for k in range(2)]
    last = len(units) - 1
    out_pieces = [(1, 2), (2, chunks - 2), (chunks - 2, chunks - 1), (chunks - 1, chunks)]
    early = 2
    lead = 2
    pieces = [[(0, chunks - 1), (chunks - 1, chunks)] for _ in range(early)]
    pieces += [[(0, chunks)] for _ in range(early, groups - 1)]
    pieces += [[(0, chunks - 1), (chunks - 1, chunks)]]

    def field_copy(which, f):
        source, target = ((field_hbm, field_ref), (flow_hbm, flow_ref))[which]
        span = pl.ds(f * orders_half, orders_half)
        return pltpu.make_async_copy(source.at[:, span], target.at[:, span], field_sem.at[which, f])

    def first_table(f):
        span = pl.ds(f * orders_half, orders_half)
        return pltpu.make_async_copy(
            table_hbm.at[span, :, pl.ds(0, width)], table_ref.at[0, span], table_sem.at[f]
        )

    def table_copy(chunk):
        return pltpu.make_async_copy(
            table_hbm.at[:, :, pl.ds(chunk * width, width)], table_ref.at[chunk],
            table_sem.at[halves + chunk - 1],
        )

    small = [
        pltpu.make_async_copy(source, target, small_sem.at[k])
        for k, (source, target) in enumerate(
            ((kappa_hbm, kappa_ref), (synth_hbm, synth_ref), (analysis_hbm, analysis_ref))
        )
    ]

    def load_half(f):
        field_copy(0, f).start()
        field_copy(1, f).start()
        first_table(f).start()

    load_half(0)
    barrier = pltpu.get_barrier_semaphore()
    for hop in range(1, parts):
        pl.semaphore_signal(
            barrier, inc=1, device_id={"mode": lax.rem(me + hop, parts)},
            device_id_type=pl.DeviceIdType.MESH,
        )
    for hop in range(1, rings):
        pl.semaphore_signal(
            barrier, inc=1, device_id={"radial": lax.rem(ring + hop, rings)},
            device_id_type=pl.DeviceIdType.MESH,
        )
    for f in range(1, halves):
        load_half(f)
    for chunk in range(1, chunks):
        table_copy(chunk).start()
    for copy in small:
        copy.start()

    def exchange(axis, to, source, target, send, receive):
        return pltpu.make_async_remote_copy(
            src_ref=source, dst_ref=target, send_sem=send, recv_sem=receive,
            device_id={axis: to}, device_id_type=pl.DeviceIdType.MESH,
        )

    def first_copy(f, hop, slot):
        to = lax.rem(me + hop, parts)
        return exchange(
            "mode", to, send_ref.at[to, 0, f], recv_ref.at[slot, 0, f],
            send_sem.at[f, hop - 1], recv_sem.at[f, hop - 1],
        )

    def lat_copy(piece, hop, slot):
        to = lax.rem(me + hop, parts)
        first, end = out_pieces[piece]
        span = pl.ds(first, end - first)
        at = halves + piece
        return exchange(
            "mode", to, send_ref.at[to, span], recv_ref.at[slot, span],
            send_sem.at[at, hop - 1], recv_sem.at[at, hop - 1],
        )

    def lat_copies(piece, hop, slot):
        return [first_copy(f, hop, slot) for f in range(halves)] if piece < 0 else [lat_copy(piece, hop, slot)]

    def back_copy(group, piece, hop, slot):
        to = lax.rem(me + hop, parts)
        first, end = pieces[group][piece]
        at = sum(len(p) for p in pieces[:group]) + piece
        span = pl.ds(first, end - first)
        return exchange(
            "mode", to, back_send_ref.at[group, to, span], back_recv_ref.at[group, slot, span],
            back_send_sem.at[at, hop - 1], back_recv_sem.at[at, hop - 1],
        )

    def send_back(group, piece):
        for hop in range(1, parts):
            back_copy(group, piece, hop, me).start()

    def edge_buffers(unit):
        return (edge_ref.at[unit], edges_ref.at[unit]) if unit < pairs - 1 else (
            half_edge_ref.at[unit - pairs + 1], half_edges_ref.at[unit - pairs + 1]
        )

    def edge_copy(unit, hop, slot):
        here, there = edge_buffers(unit)
        return exchange(
            "radial", partner(ring, hop, rings), here, there.at[slot],
            edge_send_sem.at[unit, hop - 1], edge_recv_sem.at[unit, hop - 1],
        )

    def slope_copy(hop, slot):
        return exchange(
            "radial", partner(ring, hop, rings), slope_ref, slopes_ref.at[slot],
            slope_send_sem.at[hop - 1], slope_recv_sem.at[hop - 1],
        )

    def stack(order, carry):
        spectral_ref[order] = jnp.concatenate(
            [ref[:, order, half, :] for half in range(2) for ref in (field_ref, flow_ref)], axis=0
        ).astype(jnp.bfloat16)
        return carry

    def transform_of(chunk):
        def transform(order, carry):
            base = pl.multiple_of(order * count, count)
            rows_ref[pl.ds(base, count), :] = jnp.dot(
                spectral_ref[order], table_ref[chunk, order], preferred_element_type=jnp.float32
            )
            return carry

        return transform

    def picked(row, f):
        values = rows_ref[pl.ds(row + f * orders_half * count, wide_rows, stride=2 * shells), :]
        return values.astype(jnp.bfloat16)

    def pack_of(chunk, f):
        def pack(row, carry):
            which, shell = row // shells, row % shells
            send_ref[shell // mine, chunk, f, which, shell % mine] = picked(row, f)
            return carry

        return pack

    def pack_for(to, target, f):
        def pack(row, carry):
            which, local = row // mine, row % mine
            target[to, 0, f, which, local] = picked(which * shells + to * mine + local, f)
            return carry

        lax.fori_loop(0, 2 * mine, pack, 0, unroll=8)

    for f in range(halves):
        field_copy(0, f).wait()
        field_copy(1, f).wait()
        low, high = f * orders_half, (f + 1) * orders_half
        lax.fori_loop(low, high, stack, 0, unroll=4)
        first_table(f).wait()
        lax.fori_loop(low, high, transform_of(0), 0, unroll=4)
        for hop in range(1, parts):
            pack_for(lax.rem(me + hop, parts), send_ref, f)
            if f == 0 and hop == 1:
                pl.semaphore_wait(barrier, parts + rings - 2)
            first_copy(f, hop, me).start()
        pack_for(me, recv_ref, f)
    for piece, (first, end) in enumerate(out_pieces):
        for chunk in range(first, end):
            table_copy(chunk).wait()
            lax.fori_loop(0, ord_dev, transform_of(chunk), 0, unroll=4)
            for f in range(halves):
                lax.fori_loop(0, 2 * shells, pack_of(chunk, f), 0, unroll=8)
            recv_ref[me, chunk] = send_ref[me, chunk]
        for hop in range(1, parts):
            lat_copy(piece, hop, me).start()

    for copy in small:
        copy.wait()
    offset = nr_total * 7 // 13
    cut = [slice(block * 128, (block + 1) * 128) for block in range(blocks)]
    tile = (full, 128)
    tiles = [(pair, block) for pair in range(pairs) for block in range(blocks)]
    blank = jnp.zeros(tile, jnp.float32)
    unity = jnp.ones(tile, jnp.float32)

    def angular(pair, block):
        degree = (
            me * ord_dev
            + pair * 2 * per
            + block * 128
            + lax.broadcasted_iota(jnp.int32, tile, 0) // 2
            + lax.broadcasted_iota(jnp.int32, tile, 1)
        ).astype(jnp.float32)
        return degree * (degree + 1.0)

    angulars = [angular(pair, block) for pair, block in tiles]

    def factor(shell, carry):
        kappa = jnp.full(tile, kappa_ref[shell], jnp.float32)
        spot = jnp.full(tile, ring * shells + shell, jnp.int32)
        lower = jnp.where(spot > 0, -kappa, 0.0)
        upper = jnp.where(spot < nr_total - 1, -kappa, 0.0)
        radius = (offset + spot).astype(jnp.float32)
        weight = kappa / (radius * radius)
        new = []
        for k, (pair, block) in enumerate(tiles):
            ratio, pull, weighed = carry[k]
            first_ref[pair, shell, :, cut[block]] = weighed
            diagonal = 1.0 + 2.0 * kappa + weight * angulars[k]
            inverse = 1.0 / (diagonal - lower * ratio)
            ratio = upper * inverse
            pull = -lower * pull * inverse
            inverse_ref[pair, shell, :, cut[block]] = inverse
            ratio_ref[pair, shell, :, cut[block]] = ratio
            beta_ref[pair, shell, :, cut[block]] = pull
            new.append((ratio, pull, -ratio * weighed))
        return tuple(new)

    lax.fori_loop(0, shells, factor, tuple((blank, unity, unity) for _ in tiles))

    def unfactor(step, carry):
        shell = shells - 1 - step
        spot = jnp.full(tile, ring * shells + shell, jnp.int32)
        pushed = jnp.where(spot > 0, jnp.full(tile, kappa_ref[shell], jnp.float32), 0.0)
        new = []
        for k, (pair, block) in enumerate(tiles):
            beta, gamma, to_first, to_end = carry[k]
            inverse = inverse_ref[pair, shell, :, cut[block]]
            to_first = inverse * (first_ref[pair, shell, :, cut[block]] + to_first)
            to_end = inverse * to_end
            first_ref[pair, shell, :, cut[block]] = to_first
            end_ref[pair, shell, :, cut[block]] = to_end
            ratio = ratio_ref[pair, shell, :, cut[block]]
            beta = beta_ref[pair, shell, :, cut[block]] - ratio * beta
            gamma = -ratio * gamma
            beta_ref[pair, shell, :, cut[block]] = beta
            gamma_ref[pair, shell, :, cut[block]] = gamma
            new.append((beta, gamma, pushed * to_first, pushed * to_end))
        return tuple(new)

    lax.fori_loop(0, shells, unfactor, tuple((blank, unity, blank, unity) for _ in tiles))
    for pair in range(pairs):
        for side, shell in enumerate((0, shells - 1)):
            slope_ref[2 * side, pair] = beta_ref[pair, shell]
            slope_ref[2 * side + 1, pair] = gamma_ref[pair, shell]
    slopes_ref[ring] = slope_ref[...]
    for hop in range(1, rings):
        slope_copy(hop, ring).start()

    def multiply_of(chunk):
        def back_of(locals_):
            grids = []
            for which in range(2):
                lat = jnp.concatenate(
                    [
                        jnp.concatenate(
                            [
                                recv_ref[part, chunk, f, which, local]
                                for part in range(parts)
                                for f in range(halves)
                            ],
                            axis=0,
                        )
                        for local in locals_
                    ],
                    axis=1,
                )
                grids.append(jnp.dot(synth_ref[...], lat, preferred_element_type=jnp.float32))
            product = (grids[0] * grids[1]).astype(jnp.bfloat16)
            return jnp.dot(analysis_ref[...], product, preferred_element_type=jnp.float32) * scale

        def multiply(step, carry):
            backs = [back_of((step * 4 + 2 * k, step * 4 + 2 * k + 1)) for k in range(2)]
            for part in range(parts):
                for group in range(groups):
                    base = (part * groups + group) * rows
                    back_send_ref[group, part, chunk, step] = jnp.concatenate(
                        [back[base : base + rows, k * width : (k + 1) * width] for back in backs for k in range(2)],
                        axis=0,
                    ).astype(jnp.bfloat16)
            return carry

        return multiply

    for piece in range(-1, len(out_pieces)):
        for hop in range(1, parts):
            for copy in lat_copies(piece, hop, lax.rem(me + parts - hop, parts)):
                copy.wait_recv()
        first, end = (0, 1) if piece < 0 else out_pieces[piece]
        for chunk in range(first, end):
            lax.fori_loop(0, mine // 4, multiply_of(chunk), 0)
        if end >= chunks - 1:
            for group in range(early):
                send_back(group, end - chunks + 1)
    for group in range(early, units[lead - 1][0][-1] + 1):
        for piece in range(len(pieces[group])):
            send_back(group, piece)
    for group in range(groups):
        back_recv_ref[group, me] = back_send_ref[group, me]

    for hop in range(1, rings):
        slope_copy(hop, partner(ring, hop, rings)).wait_recv()
    for pair, block in tiles:
        slope = blank
        for device in range(rings):
            head0, head1, tail0, tail1 = [slopes_ref[device, k, pair, :, cut[block]] for k in range(4)]
            inverse = 1.0 / (1.0 - head0 * slope)
            gain = head1 * inverse
            carried = tail0 * slope * inverse
            for k, value in enumerate((inverse, head0 * inverse, gain, carried, tail0 + carried * head0, slope)):
                chain_ref[pair, device, k, :, cut[block]] = value
            slope = tail1 + tail0 * slope * gain

    def widen(group, first, end):
        for chunk in range(first, end):
            for part in range(parts):
                for step in range(mine // 4):
                    base = (part * mine + 4 * step) * rows
                    wide_ref[chunk, base : base + 4 * rows, :] = back_recv_ref[
                        group, part, chunk, step
                    ].astype(jnp.float32)

    def untransform(group, first, end):
        for local in range(per):
            order = group * per + local
            stacked = jnp.concatenate(
                [
                    jnp.concatenate(
                        [
                            wide_ref[chunk, pl.ds(2 * local + half, shells, stride=rows), :].astype(jnp.bfloat16)
                            for chunk in range(first, end)
                        ],
                        axis=1,
                    )
                    for half in range(2)
                ],
                axis=0,
            )
            table = jnp.concatenate([table_ref[chunk, order] for chunk in range(first, end)], axis=1)
            forcing = lax.dot_general(
                stacked, table, (((1,), (1,)), ((), ())), preferred_element_type=jnp.float32
            )
            if first > 0:
                forcing = sum_ref[local] + forcing
            if end < chunks:
                sum_ref[local] = forcing
                continue
            for half in range(2):
                right = field_ref[:, order, half, :] + forcing[half * shells : (half + 1) * shells]
                row = (group % 2) * rows + 2 * local + half
                for block in range(blocks):
                    right_ref[block, pl.ds(row, shells, stride=full), :] = right[:, cut[block]]

    def send_edges(unit):
        _, pair, low, high = units[unit]
        size = high - low

        def gather(shell, carry):
            new = []
            for block in range(blocks):
                right = right_ref[block, pl.ds(pl.multiple_of(shell * full, full) + low, size), :]
                for side, weights in enumerate((first_ref, end_ref)):
                    new.append(carry[2 * block + side] + right * weights[pair, shell, low:high, cut[block]])
            return tuple(new)

        zeros = tuple(jnp.zeros((size, 128), jnp.float32) for _ in range(2 * blocks))
        sums = lax.fori_loop(0, shells, gather, zeros, unroll=8)
        here, there = edge_buffers(unit)
        for block in range(blocks):
            for side in range(2):
                here[side * size : (side + 1) * size, cut[block]] = sums[2 * block + side]
        for hop in reversed(range(1, rings)):
            edge_copy(unit, hop, ring).start()
        there[ring] = here[...]

    def solve(unit):
        _, pair, low, high = units[unit]
        empty = tuple(jnp.zeros((high - low, 128), jnp.float32) for _ in range(blocks))

        def forward(shell, carry):
            index = ring * shells + shell
            lower = jnp.where(jnp.full(empty[0].shape, index, jnp.int32) > 0, -kappa_ref[shell], 0.0)
            start = shell * full
            new = []
            for block in range(blocks):
                right = right_ref[block, pl.ds(pl.multiple_of(start, full) + low, high - low), :]
                value = (right - lower * carry[block]) * inverse_ref[pair, shell, low:high, cut[block]]
                alpha_ref[pair, shell, low:high, cut[block]] = value
                new.append(value)
            return tuple(new)

        lax.fori_loop(0, shells, forward, empty, unroll=4)

        def backward(step, carry):
            shell = shells - 1 - step
            new = []
            for block in range(blocks):
                value = (
                    alpha_ref[pair, shell, low:high, cut[block]]
                    - ratio_ref[pair, shell, low:high, cut[block]] * carry[block]
                )
                alpha_ref[pair, shell, low:high, cut[block]] = value
                new.append(value)
            return tuple(new)

        lax.fori_loop(0, shells, backward, empty, unroll=4)
    def finish(unit):
        members, pair, low, high = units[unit]
        size = high - low
        for hop in reversed(range(1, rings)):
            edge_copy(unit, hop, partner(ring, hop, rings)).wait_recv()
        _, there = edge_buffers(unit)
        empty = jnp.zeros((size, 128), jnp.float32)
        spot = jnp.full((size, 128), ring, jnp.int32)
        befores, afters = [], []
        for block in range(blocks):
            known, consts, left, tilt = empty, [], empty, empty
            for device in range(rings):
                first, end = [there[device, side * size : (side + 1) * size, cut[block]] for side in range(2)]
                inverse, headed, _, carried, through, slope = [
                    chain_ref[pair, device, k, low:high, cut[block]] for k in range(6)
                ]
                here = spot == device
                left = jnp.where(here, known, left)
                tilt = jnp.where(here, slope, tilt)
                consts.append(inverse * first + headed * known)
                known = end + carried * first + through * known
            beyond, before, after = empty, empty, empty
            for device in reversed(range(rings)):
                here = spot == device
                start = consts[device] + chain_ref[pair, device, 2, low:high, cut[block]] * beyond
                before = jnp.where(here, left + tilt * start, before)
                after = jnp.where(here, beyond, after)
                beyond = start
            befores.append(before)
            afters.append(after)

        def emit(shell, carry):
            for block in range(blocks):
                value = (
                    alpha_ref[pair, shell, low:high, cut[block]]
                    + beta_ref[pair, shell, low:high, cut[block]] * befores[block]
                    + gamma_ref[pair, shell, low:high, cut[block]] * afters[block]
                )
                for k in range(size // 2):
                    out_ref[shell, members[0] * per + k, :, cut[block]] = value[2 * k : 2 * k + 2]
            return carry

        lax.fori_loop(0, shells, emit, 0, unroll=4)

    def settle(unit):
        for group in units[unit][0]:
            for piece in range(len(pieces[group])):
                for hop in range(1, parts):
                    back_copy(group, piece, hop, me).wait_send()

    for unit, (members, _, _, _) in enumerate(units):
        for group in members:
            for piece, (first, end) in enumerate(pieces[group]):
                for hop in range(1, parts):
                    back_copy(group, piece, hop, lax.rem(me + parts - hop, parts)).wait_recv()
                if unit == last:
                    widen(group, first, end)
                    untransform(group, first, end)
        if unit + lead <= last:
            for group in units[unit + lead][0]:
                for piece in range(len(pieces[group])):
                    send_back(group, piece)
        if unit < last:
            for group in members:
                widen(group, 0, chunks)
                untransform(group, 0, chunks)
        send_edges(unit)
        solve(unit)
        if unit == 0:
            for hop in range(1, parts):
                for piece in range(-1, len(out_pieces)):
                    for copy in lat_copies(piece, hop, me):
                        copy.wait_send()
            for hop in range(1, rings):
                slope_copy(hop, ring).wait_send()
        else:
            finish(unit - 1)
            settle(unit - 1)
            for hop in range(1, rings):
                edge_copy(unit - 1, hop, ring).wait_send()
    settle(last)
    finish(last)
    for hop in range(1, rings):
        edge_copy(last, hop, ring).wait_send()


def on_device(scalar_field, radial_flow, legendre, diffusivity):
    shells, ord_dev, _, degrees = scalar_field.shape
    lats = legendre.shape[2]
    parts, rings = lax.axis_size("mode"), lax.axis_size("radial")
    mine = shells // parts
    synth, analysis, scale = longitude_tables(ord_dev * parts)
    width, per, orders_half = 128, 2, 8
    chunks, blocks = lats // width, degrees // 128
    halves, groups = ord_dev // orders_half, ord_dev // per
    pairs, full = groups // 2, 4 * per
    assert rings & (rings - 1) == 0 and mine % 4 == 0 and chunks >= 5
    assert lats % width == 0 and degrees % 128 == 0 and ord_dev % orders_half == 0
    bf16, f32 = jnp.bfloat16, jnp.float32
    vmem, hbm = pl.BlockSpec(memory_space=pltpu.VMEM), pl.BlockSpec(memory_space=pltpu.HBM)
    dma = pltpu.SemaphoreType.DMA
    solved = pltpu.VMEM((pairs, shells, full, degrees), f32)
    there = pltpu.VMEM((parts, chunks, halves, 2, mine, 2 * orders_half, width), bf16)
    back = pltpu.VMEM((groups, parts, chunks, mine // 4, 8 * per, width), bf16)
    return pl.pallas_call(
        functools.partial(whole_step, scale),
        in_specs=[hbm] * 6,
        out_specs=vmem,
        out_shape=pltpu.VMEM(scalar_field.shape, f32),
        scratch_shapes=[
            pltpu.SMEM(diffusivity.shape, f32),
            pltpu.VMEM(synth.shape, bf16),
            pltpu.VMEM(analysis.shape, bf16),
            pltpu.VMEM(scalar_field.shape, f32),
            pltpu.VMEM(scalar_field.shape, f32),
            pltpu.VMEM((chunks, ord_dev, degrees, width), bf16),
            pltpu.VMEM((ord_dev, 4 * shells, degrees), bf16),
            pltpu.VMEM((4 * shells * ord_dev, width), f32),
            there, there, back, back,
            pltpu.VMEM((chunks, shells * 2 * per, width), f32),
            pltpu.VMEM((per, 2 * shells, degrees), f32),
            pltpu.VMEM((blocks, shells * full, 128), f32),
            solved, solved, solved, solved, solved, solved, solved,
            pltpu.VMEM((4, pairs, full, degrees), f32),
            pltpu.VMEM((rings, 4, pairs, full, degrees), f32),
            pltpu.VMEM((pairs, rings, 6, full, degrees), f32),
            pltpu.VMEM((pairs - 1, 2 * full, degrees), f32),
            pltpu.VMEM((pairs - 1, rings, 2 * full, degrees), f32),
            pltpu.VMEM((2, full, degrees), f32),
            pltpu.VMEM((2, rings, full, degrees), f32),
            dma((3,)),
            dma((2, halves)),
            dma((halves + chunks - 1,)),
            dma((halves + 4, parts - 1)),
            dma((halves + 4, parts - 1)),
            dma((groups + 3, parts - 1)),
            dma((groups + 3, parts - 1)),
            dma((rings - 1,)),
            dma((rings - 1,)),
            dma((pairs + 1, rings - 1)),
            dma((pairs + 1, rings - 1)),
        ],
        compiler_params=params(collective_id=0, has_side_effects=True),
        name="whole_step",
    )(diffusivity, legendre, scalar_field, radial_flow, synth, analysis)


def solution(mesh):
    return jax.shard_map(
        on_device,
        mesh=mesh,
        in_specs=(
            P("radial", "mode", None, None),
            P("radial", "mode", None, None),
            P("mode", None, None),
            P("radial"),
        ),
        out_specs=P("radial", "mode", None, None),
        check_vma=False,
    )
```

```python
import functools
import math

import jax
import jax.numpy as jnp
import numpy as np
from jax import lax
from jax.experimental import pallas as pl
from jax.experimental.pallas import tpu as pltpu
from jax.sharding import PartitionSpec as P

NLON = 1536
VMEM_LIMIT = 56 * 1024 * 1024


def params(**more):
    return pltpu.CompilerParams(vmem_limit_bytes=VMEM_LIMIT, **more)


def grid_points(orders):
    needed = 3 * (orders - 1) + 1
    return next(q for q in range(128, NLON + 1, 128) if q >= needed and NLON % q == 0)


def longitude_tables(orders):
    points = grid_points(orders)
    stride = NLON // points
    phase = np.arange(orders)[:, None] * (np.arange(points) * stride)[None, :] % NLON
    angle = phase.astype(np.float32) * np.float32(2.0 * math.pi / NLON)
    paired = np.stack([np.cos(angle), -np.sin(angle)], axis=1).reshape(2 * orders, points)
    synth = (paired / np.float32(math.sqrt(orders))).astype(jnp.bfloat16)
    analysis = (paired * np.float32(math.sqrt(2.0 / NLON))).astype(jnp.bfloat16)
    return jnp.asarray(synth.T), jnp.asarray(analysis), float(stride)


def partner(here, hop, size):
    place, bit = 0, 1
    while bit < size:
        place = place + (here // bit + hop // bit) % 2 * bit
        bit *= 2
    return place


def whole_step(
    scale, kappa_hbm, table_hbm, field_hbm, flow_hbm, synth_hbm, analysis_hbm, out_ref,
    kappa_ref, synth_ref, analysis_ref, field_ref, flow_ref, table_ref, spectral_ref, rows_ref,
    send_ref, recv_ref, back_send_ref, back_recv_ref,
    wide_ref, right_ref, alpha_ref, beta_ref, gamma_ref, ratio_ref, inverse_ref, first_ref, end_ref,
    slope_ref, slopes_ref, chain_ref, edge_ref, edges_ref, half_edge_ref, half_edges_ref,
    small_sem, field_sem, table_sem, send_sem, recv_sem, back_send_sem, back_recv_sem,
    slope_send_sem, slope_recv_sem, edge_send_sem, edge_recv_sem,
):
    shells, ord_dev, _, degrees = field_ref.shape
    parts, rings = lax.axis_size("mode"), lax.axis_size("radial")
    me, ring = lax.axis_index("mode"), lax.axis_index("radial")
    mine = shells // parts
    count = 4 * shells
    width = 128
    blocks = degrees // 128
    nr_total = shells * rings
    chunks, halves, wide_rows = send_ref.shape[1], send_ref.shape[2], send_ref.shape[5]
    orders_half = ord_dev // halves
    groups = back_send_ref.shape[0]
    per = ord_dev // groups
    rows = 2 * per
    pairs, full = groups // 2, 2 * rows
    units = [((2 * pair, 2 * pair + 1), pair, 0, full) for pair in range(pairs - 1)]
    units += [((groups - 2 + k,), pairs - 1, k * rows, (k + 1) * rows) for k in range(2)]
    last = len(units) - 1
    out_pieces = [(1, chunks // 2), (chunks // 2, chunks - 1), (chunks - 1, chunks)]
    early = 2
    lead = 2
    pieces = [[(0, chunks - 1), (chunks - 1, chunks)] for _ in range(early)]
    pieces += [[(0, chunks)] for _ in range(early, groups)]

    def field_copy(which, f):
        source, target = ((field_hbm, field_ref), (flow_hbm, flow_ref))[which]
        span = pl.ds(f * orders_half, orders_half)
        return pltpu.make_async_copy(source.at[:, span], target.at[:, span], field_sem.at[which, f])

    def first_table(f):
        span = pl.ds(f * orders_half, orders_half)
        return pltpu.make_async_copy(
            table_hbm.at[span, :, pl.ds(0, width)], table_ref.at[0, span], table_sem.at[f]
        )

    def table_copy(chunk):
        return pltpu.make_async_copy(
            table_hbm.at[:, :, pl.ds(chunk * width, width)], table_ref.at[chunk],
            table_sem.at[halves + chunk - 1],
        )

    small = [
        pltpu.make_async_copy(source, target, small_sem.at[k])
        for k, (source, target) in enumerate(
            ((kappa_hbm, kappa_ref), (synth_hbm, synth_ref), (analysis_hbm, analysis_ref))
        )
    ]

    def load_half(f):
        field_copy(0, f).start()
        field_copy(1, f).start()
        first_table(f).start()

    load_half(0)
    barrier = pltpu.get_barrier_semaphore()
    for hop in range(1, parts):
        pl.semaphore_signal(
            barrier, inc=1, device_id={"mode": lax.rem(me + hop, parts)},
            device_id_type=pl.DeviceIdType.MESH,
        )
    for hop in range(1, rings):
        pl.semaphore_signal(
            barrier, inc=1, device_id={"radial": lax.rem(ring + hop, rings)},
            device_id_type=pl.DeviceIdType.MESH,
        )
    for f in range(1, halves):
        load_half(f)
    for chunk in range(1, chunks):
        table_copy(chunk).start()
    for copy in small:
        copy.start()

    def exchange(axis, to, source, target, send, receive):
        return pltpu.make_async_remote_copy(
            src_ref=source, dst_ref=target, send_sem=send, recv_sem=receive,
            device_id={axis: to}, device_id_type=pl.DeviceIdType.MESH,
        )

    def first_copy(f, hop, slot):
        to = lax.rem(me + hop, parts)
        return exchange(
            "mode", to, send_ref.at[to, 0, f], recv_ref.at[slot, 0, f],
            send_sem.at[f, hop - 1], recv_sem.at[f, hop - 1],
        )

    def lat_copy(piece, hop, slot):
        to = lax.rem(me + hop, parts)
        first, end = out_pieces[piece]
        span = pl.ds(first, end - first)
        at = halves + piece
        return exchange(
            "mode", to, send_ref.at[to, span], recv_ref.at[slot, span],
            send_sem.at[at, hop - 1], recv_sem.at[at, hop - 1],
        )

    def lat_copies(piece, hop, slot):
        return [first_copy(f, hop, slot) for f in range(halves)] if piece < 0 else [lat_copy(piece, hop, slot)]

    def back_copy(group, piece, hop, slot):
        to = lax.rem(me + hop, parts)
        first, end = pieces[group][piece]
        at = sum(len(p) for p in pieces[:group]) + piece
        span = pl.ds(first, end - first)
        return exchange(
            "mode", to, back_send_ref.at[group, to, span], back_recv_ref.at[group, slot, span],
            back_send_sem.at[at, hop - 1], back_recv_sem.at[at, hop - 1],
        )

    def send_back(group, piece):
        for hop in range(1, parts):
            back_copy(group, piece, hop, me).start()

    def edge_buffers(unit):
        return (edge_ref.at[unit], edges_ref.at[unit]) if unit < pairs - 1 else (
            half_edge_ref.at[unit - pairs + 1], half_edges_ref.at[unit - pairs + 1]
        )

    def edge_copy(unit, hop, slot):
        here, there = edge_buffers(unit)
        return exchange(
            "radial", partner(ring, hop, rings), here, there.at[slot],
            edge_send_sem.at[unit, hop - 1], edge_recv_sem.at[unit, hop - 1],
        )

    def slope_copy(hop, slot):
        return exchange(
            "radial", partner(ring, hop, rings), slope_ref, slopes_ref.at[slot],
            slope_send_sem.at[hop - 1], slope_recv_sem.at[hop - 1],
        )

    def stack(order, carry):
        spectral_ref[order] = jnp.concatenate(
            [ref[:, order, half, :] for half in range(2) for ref in (field_ref, flow_ref)], axis=0
        ).astype(jnp.bfloat16)
        return carry

    def transform_of(chunk):
        def transform(order, carry):
            base = pl.multiple_of(order * count, count)
            rows_ref[pl.ds(base, count), :] = jnp.dot(
                spectral_ref[order], table_ref[chunk, order], preferred_element_type=jnp.float32
            )
            return carry

        return transform

    def picked(row, f):
        values = rows_ref[pl.ds(row + f * orders_half * count, wide_rows, stride=2 * shells), :]
        return values.astype(jnp.bfloat16)

    def pack_of(chunk, f):
        def pack(row, carry):
            which, shell = row // shells, row % shells
            send_ref[shell // mine, chunk, f, which, shell % mine] = picked(row, f)
            return carry

        return pack

    def pack_for(to, target, f):
        def pack(row, carry):
            which, local = row // mine, row % mine
            target[to, 0, f, which, local] = picked(which * shells + to * mine + local, f)
            return carry

        lax.fori_loop(0, 2 * mine, pack, 0, unroll=8)

    for f in range(halves):
        field_copy(0, f).wait()
        field_copy(1, f).wait()
        low, high = f * orders_half, (f + 1) * orders_half
        lax.fori_loop(low, high, stack, 0, unroll=4)
        first_table(f).wait()
        lax.fori_loop(low, high, transform_of(0), 0, unroll=4)
        for hop in range(1, parts):
            pack_for(lax.rem(me + hop, parts), send_ref, f)
            if f == 0 and hop == 1:
                pl.semaphore_wait(barrier, parts + rings - 2)
            first_copy(f, hop, me).start()
        pack_for(me, recv_ref, f)
    for piece, (first, end) in enumerate(out_pieces):
        for chunk in range(first, end):
            table_copy(chunk).wait()
            lax.fori_loop(0, ord_dev, transform_of(chunk), 0, unroll=4)
            for f in range(halves):
                lax.fori_loop(0, 2 * shells, pack_of(chunk, f), 0, unroll=8)
            recv_ref[me, chunk] = send_ref[me, chunk]
        for hop in range(1, parts):
            lat_copy(piece, hop, me).start()

    for copy in small:
        copy.wait()
    offset = nr_total * 7 // 13
    cut = [slice(block * 128, (block + 1) * 128) for block in range(blocks)]
    tile = (full, 128)
    tiles = [(pair, block) for pair in range(pairs) for block in range(blocks)]
    blank = jnp.zeros(tile, jnp.float32)
    unity = jnp.ones(tile, jnp.float32)

    def angular(pair, block):
        degree = (
            me * ord_dev
            + pair * 2 * per
            + block * 128
            + lax.broadcasted_iota(jnp.int32, tile, 0) // 2
            + lax.broadcasted_iota(jnp.int32, tile, 1)
        ).astype(jnp.float32)
        return degree * (degree + 1.0)

    angulars = [angular(pair, block) for pair, block in tiles]

    def factor(shell, carry):
        kappa = jnp.full(tile, kappa_ref[shell], jnp.float32)
        spot = jnp.full(tile, ring * shells + shell, jnp.int32)
        lower = jnp.where(spot > 0, -kappa, 0.0)
        upper = jnp.where(spot < nr_total - 1, -kappa, 0.0)
        radius = (offset + spot).astype(jnp.float32)
        weight = kappa / (radius * radius)
        new = []
        for k, (pair, block) in enumerate(tiles):
            ratio, pull, weighed = carry[k]
            first_ref[pair, shell, :, cut[block]] = weighed
            diagonal = 1.0 + 2.0 * kappa + weight * angulars[k]
            inverse = 1.0 / (diagonal - lower * ratio)
            ratio = upper * inverse
            pull = -lower * pull * inverse
            inverse_ref[pair, shell, :, cut[block]] = inverse
            ratio_ref[pair, shell, :, cut[block]] = ratio
            beta_ref[pair, shell, :, cut[block]] = pull
            new.append((ratio, pull, -ratio * weighed))
        return tuple(new)

    lax.fori_loop(0, shells, factor, tuple((blank, unity, unity) for _ in tiles))

    def unfactor(step, carry):
        shell = shells - 1 - step
        spot = jnp.full(tile, ring * shells + shell, jnp.int32)
        pushed = jnp.where(spot > 0, jnp.full(tile, kappa_ref[shell], jnp.float32), 0.0)
        new = []
        for k, (pair, block) in enumerate(tiles):
            beta, gamma, to_first, to_end = carry[k]
            inverse = inverse_ref[pair, shell, :, cut[block]]
            to_first = inverse * (first_ref[pair, shell, :, cut[block]] + to_first)
            to_end = inverse * to_end
            first_ref[pair, shell, :, cut[block]] = to_first
            end_ref[pair, shell, :, cut[block]] = to_end
            ratio = ratio_ref[pair, shell, :, cut[block]]
            beta = beta_ref[pair, shell, :, cut[block]] - ratio * beta
            gamma = -ratio * gamma
            beta_ref[pair, shell, :, cut[block]] = beta
            gamma_ref[pair, shell, :, cut[block]] = gamma
            new.append((beta, gamma, pushed * to_first, pushed * to_end))
        return tuple(new)

    lax.fori_loop(0, shells, unfactor, tuple((blank, unity, blank, unity) for _ in tiles))
    for pair in range(pairs):
        for side, shell in enumerate((0, shells - 1)):
            slope_ref[2 * side, pair] = beta_ref[pair, shell]
            slope_ref[2 * side + 1, pair] = gamma_ref[pair, shell]
    slopes_ref[ring] = slope_ref[...]
    for hop in range(1, rings):
        slope_copy(hop, ring).start()

    def multiply_of(chunk):
        def back_of(locals_):
            grids = []
            for which in range(2):
                lat = jnp.concatenate(
                    [
                        jnp.concatenate(
                            [
                                recv_ref[part, chunk, f, which, local]
                                for part in range(parts)
                                for f in range(halves)
                            ],
                            axis=0,
                        )
                        for local in locals_
                    ],
                    axis=1,
                )
                grids.append(jnp.dot(synth_ref[...], lat, preferred_element_type=jnp.float32))
            product = (grids[0] * grids[1]).astype(jnp.bfloat16)
            return jnp.dot(analysis_ref[...], product, preferred_element_type=jnp.float32) * scale

        def multiply(step, carry):
            backs = [back_of((step * 4 + 2 * k, step * 4 + 2 * k + 1)) for k in range(2)]
            for part in range(parts):
                for group in range(groups):
                    base = (part * groups + group) * rows
                    back_send_ref[group, part, chunk, step] = jnp.concatenate(
                        [back[base : base + rows, k * width : (k + 1) * width] for back in backs for k in range(2)],
                        axis=0,
                    ).astype(jnp.bfloat16)
            return carry

        return multiply

    for piece in range(-1, len(out_pieces)):
        for hop in range(1, parts):
            for copy in lat_copies(piece, hop, lax.rem(me + parts - hop, parts)):
                copy.wait_recv()
        first, end = (0, 1) if piece < 0 else out_pieces[piece]
        for chunk in range(first, end):
            lax.fori_loop(0, mine // 4, multiply_of(chunk), 0)
        if end >= chunks - 1:
            for group in range(early):
                send_back(group, end - chunks + 1)
    for group in range(early, units[lead - 1][0][-1] + 1):
        for piece in range(len(pieces[group])):
            send_back(group, piece)
    for group in range(groups):
        back_recv_ref[group, me] = back_send_ref[group, me]

    for hop in range(1, rings):
        slope_copy(hop, partner(ring, hop, rings)).wait_recv()
    for pair, block in tiles:
        slope = blank
        for device in range(rings):
            head0, head1, tail0, tail1 = [slopes_ref[device, k, pair, :, cut[block]] for k in range(4)]
            inverse = 1.0 / (1.0 - head0 * slope)
            gain = head1 * inverse
            carried = tail0 * slope * inverse
            for k, value in enumerate((inverse, head0 * inverse, gain, carried, tail0 + carried * head0, slope)):
                chain_ref[pair, device, k, :, cut[block]] = value
            slope = tail1 + tail0 * slope * gain

    def widen(group):
        for chunk in range(chunks):
            for part in range(parts):
                for step in range(mine // 4):
                    base = (part * mine + 4 * step) * rows
                    wide_ref[chunk, base : base + 4 * rows, :] = back_recv_ref[
                        group, part, chunk, step
                    ].astype(jnp.float32)

    def untransform(group):
        for local in range(per):
            order = group * per + local
            stacked = jnp.concatenate(
                [
                    jnp.concatenate(
                        [
                            wide_ref[chunk, pl.ds(2 * local + half, shells, stride=rows), :].astype(jnp.bfloat16)
                            for chunk in range(chunks)
                        ],
                        axis=1,
                    )
                    for half in range(2)
                ],
                axis=0,
            )
            table = jnp.concatenate([table_ref[chunk, order] for chunk in range(chunks)], axis=1)
            forcing = lax.dot_general(
                stacked, table, (((1,), (1,)), ((), ())), preferred_element_type=jnp.float32
            )
            for half in range(2):
                right = field_ref[:, order, half, :] + forcing[half * shells : (half + 1) * shells]
                row = (group % 2) * rows + 2 * local + half
                for block in range(blocks):
                    right_ref[block, pl.ds(row, shells, stride=full), :] = right[:, cut[block]]

    def send_edges(unit):
        _, pair, low, high = units[unit]
        size = high - low

        def gather(shell, carry):
            new = []
            for block in range(blocks):
                right = right_ref[block, pl.ds(pl.multiple_of(shell * full, full) + low, size), :]
                for side, weights in enumerate((first_ref, end_ref)):
                    new.append(carry[2 * block + side] + right * weights[pair, shell, low:high, cut[block]])
            return tuple(new)

        zeros = tuple(jnp.zeros((size, 128), jnp.float32) for _ in range(2 * blocks))
        sums = lax.fori_loop(0, shells, gather, zeros, unroll=8)
        here, there = edge_buffers(unit)
        for block in range(blocks):
            for side in range(2):
                here[side * size : (side + 1) * size, cut[block]] = sums[2 * block + side]
        for hop in reversed(range(1, rings)):
            edge_copy(unit, hop, ring).start()
        there[ring] = here[...]

    def solve(unit):
        _, pair, low, high = units[unit]
        empty = tuple(jnp.zeros((high - low, 128), jnp.float32) for _ in range(blocks))

        def forward(shell, carry):
            index = ring * shells + shell
            lower = jnp.where(jnp.full(empty[0].shape, index, jnp.int32) > 0, -kappa_ref[shell], 0.0)
            start = shell * full
            new = []
            for block in range(blocks):
                right = right_ref[block, pl.ds(pl.multiple_of(start, full) + low, high - low), :]
                value = (right - lower * carry[block]) * inverse_ref[pair, shell, low:high, cut[block]]
                alpha_ref[pair, shell, low:high, cut[block]] = value
                new.append(value)
            return tuple(new)

        lax.fori_loop(0, shells, forward, empty, unroll=4)

        def backward(step, carry):
            shell = shells - 1 - step
            new = []
            for block in range(blocks):
                value = (
                    alpha_ref[pair, shell, low:high, cut[block]]
                    - ratio_ref[pair, shell, low:high, cut[block]] * carry[block]
                )
                alpha_ref[pair, shell, low:high, cut[block]] = value
                new.append(value)
            return tuple(new)

        lax.fori_loop(0, shells, backward, empty, unroll=4)
    def finish(unit):
        members, pair, low, high = units[unit]
        size = high - low
        for hop in reversed(range(1, rings)):
            edge_copy(unit, hop, partner(ring, hop, rings)).wait_recv()
        _, there = edge_buffers(unit)
        empty = jnp.zeros((size, 128), jnp.float32)
        spot = jnp.full((size, 128), ring, jnp.int32)
        befores, afters = [], []
        for block in range(blocks):
            known, consts, left, tilt = empty, [], empty, empty
            for device in range(rings):
                first, end = [there[device, side * size : (side + 1) * size, cut[block]] for side in range(2)]
                inverse, headed, _, carried, through, slope = [
                    chain_ref[pair, device, k, low:high, cut[block]] for k in range(6)
                ]
                here = spot == device
                left = jnp.where(here, known, left)
                tilt = jnp.where(here, slope, tilt)
                consts.append(inverse * first + headed * known)
                known = end + carried * first + through * known
            beyond, before, after = empty, empty, empty
            for device in reversed(range(rings)):
                here = spot == device
                start = consts[device] + chain_ref[pair, device, 2, low:high, cut[block]] * beyond
                before = jnp.where(here, left + tilt * start, before)
                after = jnp.where(here, beyond, after)
                beyond = start
            befores.append(before)
            afters.append(after)

        def emit(shell, carry):
            for block in range(blocks):
                value = (
                    alpha_ref[pair, shell, low:high, cut[block]]
                    + beta_ref[pair, shell, low:high, cut[block]] * befores[block]
                    + gamma_ref[pair, shell, low:high, cut[block]] * afters[block]
                )
                for k in range(size // 2):
                    out_ref[shell, members[0] * per + k, :, cut[block]] = value[2 * k : 2 * k + 2]
            return carry

        lax.fori_loop(0, shells, emit, 0, unroll=4)

    def settle(unit):
        for group in units[unit][0]:
            for piece in range(len(pieces[group])):
                for hop in range(1, parts):
                    back_copy(group, piece, hop, me).wait_send()

    for unit, (members, _, _, _) in enumerate(units):
        for group in members:
            for piece in range(len(pieces[group])):
                for hop in range(1, parts):
                    back_copy(group, piece, hop, lax.rem(me + parts - hop, parts)).wait_recv()
        if unit + lead <= last:
            for group in units[unit + lead][0]:
                for piece in range(len(pieces[group])):
                    send_back(group, piece)
        for group in members:
            widen(group)
            untransform(group)
        send_edges(unit)
        solve(unit)
        if unit == 0:
            for hop in range(1, parts):
                for piece in range(-1, len(out_pieces)):
                    for copy in lat_copies(piece, hop, me):
                        copy.wait_send()
            for hop in range(1, rings):
                slope_copy(hop, ring).wait_send()
        else:
            finish(unit - 1)
            settle(unit - 1)
            for hop in range(1, rings):
                edge_copy(unit - 1, hop, ring).wait_send()
    settle(last)
    finish(last)
    for hop in range(1, rings):
        edge_copy(last, hop, ring).wait_send()


def on_device(scalar_field, radial_flow, legendre, diffusivity):
    shells, ord_dev, _, degrees = scalar_field.shape
    lats = legendre.shape[2]
    parts, rings = lax.axis_size("mode"), lax.axis_size("radial")
    mine = shells // parts
    synth, analysis, scale = longitude_tables(ord_dev * parts)
    width, per, orders_half = 128, 2, 8
    chunks, blocks = lats // width, degrees // 128
    halves, groups = ord_dev // orders_half, ord_dev // per
    pairs, full = groups // 2, 4 * per
    assert rings & (rings - 1) == 0 and mine % 4 == 0 and chunks >= 5
    assert lats % width == 0 and degrees % 128 == 0 and ord_dev % orders_half == 0
    bf16, f32 = jnp.bfloat16, jnp.float32
    vmem, hbm = pl.BlockSpec(memory_space=pltpu.VMEM), pl.BlockSpec(memory_space=pltpu.HBM)
    dma = pltpu.SemaphoreType.DMA
    solved = pltpu.VMEM((pairs, shells, full, degrees), f32)
    there = pltpu.VMEM((parts, chunks, halves, 2, mine, 2 * orders_half, width), bf16)
    back = pltpu.VMEM((groups, parts, chunks, mine // 4, 8 * per, width), bf16)
    return pl.pallas_call(
        functools.partial(whole_step, scale),
        in_specs=[hbm] * 6,
        out_specs=vmem,
        out_shape=pltpu.VMEM(scalar_field.shape, f32),
        scratch_shapes=[
            pltpu.SMEM(diffusivity.shape, f32),
            pltpu.VMEM(synth.shape, bf16),
            pltpu.VMEM(analysis.shape, bf16),
            pltpu.VMEM(scalar_field.shape, f32),
            pltpu.VMEM(scalar_field.shape, f32),
            pltpu.VMEM((chunks, ord_dev, degrees, width), bf16),
            pltpu.VMEM((ord_dev, 4 * shells, degrees), bf16),
            pltpu.VMEM((4 * shells * ord_dev, width), f32),
            there, there, back, back,
            pltpu.VMEM((chunks, shells * 2 * per, width), f32),
            pltpu.VMEM((blocks, shells * full, 128), f32),
            solved, solved, solved, solved, solved, solved, solved,
            pltpu.VMEM((4, pairs, full, degrees), f32),
            pltpu.VMEM((rings, 4, pairs, full, degrees), f32),
            pltpu.VMEM((pairs, rings, 6, full, degrees), f32),
            pltpu.VMEM((pairs - 1, 2 * full, degrees), f32),
            pltpu.VMEM((pairs - 1, rings, 2 * full, degrees), f32),
            pltpu.VMEM((2, full, degrees), f32),
            pltpu.VMEM((2, rings, full, degrees), f32),
            dma((3,)),
            dma((2, halves)),
            dma((halves + chunks - 1,)),
            dma((halves + 3, parts - 1)),
            dma((halves + 3, parts - 1)),
            dma((groups + 2, parts - 1)),
            dma((groups + 2, parts - 1)),
            dma((rings - 1,)),
            dma((rings - 1,)),
            dma((pairs + 1, rings - 1)),
            dma((pairs + 1, rings - 1)),
        ],
        compiler_params=params(collective_id=0, has_side_effects=True),
        name="whole_step",
    )(diffusivity, legendre, scalar_field, radial_flow, synth, analysis)


def solution(mesh):
    return jax.shard_map(
        on_device,
        mesh=mesh,
        in_specs=(
            P("radial", "mode", None, None),
            P("radial", "mode", None, None),
            P("mode", None, None),
            P("radial"),
        ),
        out_specs=P("radial", "mode", None, None),
        check_vma=False,
    )
```

```python
import functools
import math

import jax
import jax.numpy as jnp
import numpy as np
from jax import lax
from jax.experimental import pallas as pl
from jax.experimental.pallas import tpu as pltpu
from jax.sharding import PartitionSpec as P

NLON = 1536
VMEM_LIMIT = 56 * 1024 * 1024


def params(**more):
    return pltpu.CompilerParams(vmem_limit_bytes=VMEM_LIMIT, **more)


def grid_points(orders):
    needed = 3 * (orders - 1) + 1
    return next(q for q in range(128, NLON + 1, 128) if q >= needed and NLON % q == 0)


def longitude_tables(orders):
    points = grid_points(orders)
    stride = NLON // points
    phase = np.arange(orders)[:, None] * (np.arange(points) * stride)[None, :] % NLON
    angle = phase.astype(np.float32) * np.float32(2.0 * math.pi / NLON)
    paired = np.stack([np.cos(angle), -np.sin(angle)], axis=1).reshape(2 * orders, points)
    synth = (paired / np.float32(math.sqrt(orders))).astype(jnp.bfloat16)
    analysis = (paired * np.float32(math.sqrt(2.0 / NLON))).astype(jnp.bfloat16)
    return jnp.asarray(synth.T), jnp.asarray(analysis), float(stride)


def partner(here, hop, size):
    place, bit = 0, 1
    while bit < size:
        place = place + (here // bit + hop // bit) % 2 * bit
        bit *= 2
    return place


def whole_step(
    scale, kappa_hbm, table_hbm, field_hbm, flow_hbm, synth_hbm, analysis_hbm, out_ref,
    kappa_ref, synth_ref, analysis_ref, field_ref, flow_ref, table_ref, spectral_ref, rows_ref,
    send_ref, recv_ref, back_send_ref, back_recv_ref,
    wide_ref, right_ref, alpha_ref, beta_ref, gamma_ref, ratio_ref, inverse_ref, first_ref, end_ref,
    slope_ref, slopes_ref, chain_ref, edge_ref, edges_ref, half_edge_ref, half_edges_ref,
    small_sem, field_sem, table_sem, send_sem, recv_sem, back_send_sem, back_recv_sem,
    slope_send_sem, slope_recv_sem, edge_send_sem, edge_recv_sem,
):
    shells, ord_dev, _, degrees = field_ref.shape
    parts, rings = lax.axis_size("mode"), lax.axis_size("radial")
    me, ring = lax.axis_index("mode"), lax.axis_index("radial")
    mine = shells // parts
    count = 4 * shells
    width = 128
    blocks = degrees // 128
    nr_total = shells * rings
    chunks, halves, wide_rows = send_ref.shape[1], send_ref.shape[2], send_ref.shape[5]
    orders_half = ord_dev // halves
    groups = back_send_ref.shape[0]
    per = ord_dev // groups
    rows = 2 * per
    pairs, full = groups // 2, 2 * rows
    units = [((2 * pair, 2 * pair + 1), pair, 0, full) for pair in range(pairs - 1)]
    units += [((groups - 2 + k,), pairs - 1, k * rows, (k + 1) * rows) for k in range(2)]
    last = len(units) - 1
    out_pieces = [(1, chunks // 2), (chunks // 2, chunks - 1), (chunks - 1, chunks)]
    early = 2
    lead = 2
    pieces = [[(0, chunks - 1), (chunks - 1, chunks)] for _ in range(early)]
    pieces += [[(0, chunks)] for _ in range(early, groups)]

    def field_copy(which, f):
        source, target = ((field_hbm, field_ref), (flow_hbm, flow_ref))[which]
        span = pl.ds(f * orders_half, orders_half)
        return pltpu.make_async_copy(source.at[:, span], target.at[:, span], field_sem.at[which, f])

    def first_table(f):
        span = pl.ds(f * orders_half, orders_half)
        return pltpu.make_async_copy(
            table_hbm.at[span, :, pl.ds(0, width)], table_ref.at[0, span], table_sem.at[f]
        )

    def table_copy(chunk):
        return pltpu.make_async_copy(
            table_hbm.at[:, :, pl.ds(chunk * width, width)], table_ref.at[chunk],
            table_sem.at[halves + chunk - 1],
        )

    small = [
        pltpu.make_async_copy(source, target, small_sem.at[k])
        for k, (source, target) in enumerate(
            ((kappa_hbm, kappa_ref), (synth_hbm, synth_ref), (analysis_hbm, analysis_ref))
        )
    ]

    def load_half(f):
        field_copy(0, f).start()
        field_copy(1, f).start()
        first_table(f).start()

    load_half(0)
    barrier = pltpu.get_barrier_semaphore()
    for hop in range(1, parts):
        pl.semaphore_signal(
            barrier, inc=1, device_id={"mode": lax.rem(me + hop, parts)},
            device_id_type=pl.DeviceIdType.MESH,
        )
    for hop in range(1, rings):
        pl.semaphore_signal(
            barrier, inc=1, device_id={"radial": lax.rem(ring + hop, rings)},
            device_id_type=pl.DeviceIdType.MESH,
        )
    for f in range(1, halves):
        load_half(f)
    for chunk in range(1, chunks):
        table_copy(chunk).start()
    for copy in small:
        copy.start()

    def exchange(axis, to, source, target, send, receive):
        return pltpu.make_async_remote_copy(
            src_ref=source, dst_ref=target, send_sem=send, recv_sem=receive,
            device_id={axis: to}, device_id_type=pl.DeviceIdType.MESH,
        )

    def first_copy(f, hop, slot):
        to = lax.rem(me + hop, parts)
        return exchange(
            "mode", to, send_ref.at[to, 0, f], recv_ref.at[slot, 0, f],
            send_sem.at[f, hop - 1], recv_sem.at[f, hop - 1],
        )

    def lat_copy(piece, hop, slot):
        to = lax.rem(me + hop, parts)
        first, end = out_pieces[piece]
        span = pl.ds(first, end - first)
        at = halves + piece
        return exchange(
            "mode", to, send_ref.at[to, span], recv_ref.at[slot, span],
            send_sem.at[at, hop - 1], recv_sem.at[at, hop - 1],
        )

    def lat_copies(piece, hop, slot):
        return [first_copy(f, hop, slot) for f in range(halves)] if piece < 0 else [lat_copy(piece, hop, slot)]

    def back_copy(group, piece, hop, slot):
        to = lax.rem(me + hop, parts)
        first, end = pieces[group][piece]
        at = sum(len(p) for p in pieces[:group]) + piece
        span = pl.ds(first, end - first)
        return exchange(
            "mode", to, back_send_ref.at[group, to, span], back_recv_ref.at[group, slot, span],
            back_send_sem.at[at, hop - 1], back_recv_sem.at[at, hop - 1],
        )

    def send_back(group, piece):
        for hop in range(1, parts):
            back_copy(group, piece, hop, me).start()

    def edge_buffers(unit):
        return (edge_ref.at[unit], edges_ref.at[unit]) if unit < pairs - 1 else (
            half_edge_ref.at[unit - pairs + 1], half_edges_ref.at[unit - pairs + 1]
        )

    def edge_copy(unit, hop, slot):
        here, there = edge_buffers(unit)
        return exchange(
            "radial", partner(ring, hop, rings), here, there.at[slot],
            edge_send_sem.at[unit, hop - 1], edge_recv_sem.at[unit, hop - 1],
        )

    def slope_copy(hop, slot):
        return exchange(
            "radial", partner(ring, hop, rings), slope_ref, slopes_ref.at[slot],
            slope_send_sem.at[hop - 1], slope_recv_sem.at[hop - 1],
        )

    def stack(order, carry):
        spectral_ref[order] = jnp.concatenate(
            [ref[:, order, half, :] for half in range(2) for ref in (field_ref, flow_ref)], axis=0
        ).astype(jnp.bfloat16)
        return carry

    def transform_of(chunk):
        def transform(order, carry):
            base = pl.multiple_of(order * count, count)
            rows_ref[pl.ds(base, count), :] = jnp.dot(
                spectral_ref[order], table_ref[chunk, order], preferred_element_type=jnp.float32
            )
            return carry

        return transform

    def picked(row, f):
        values = rows_ref[pl.ds(row + f * orders_half * count, wide_rows, stride=2 * shells), :]
        return values.astype(jnp.bfloat16)

    def pack_of(chunk, f):
        def pack(row, carry):
            which, shell = row // shells, row % shells
            send_ref[shell // mine, chunk, f, which, shell % mine] = picked(row, f)
            return carry

        return pack

    def pack_for(to, target, f):
        def pack(row, carry):
            which, local = row // mine, row % mine
            target[to, 0, f, which, local] = picked(which * shells + to * mine + local, f)
            return carry

        lax.fori_loop(0, 2 * mine, pack, 0, unroll=8)

    for f in range(halves):
        field_copy(0, f).wait()
        field_copy(1, f).wait()
        low, high = f * orders_half, (f + 1) * orders_half
        lax.fori_loop(low, high, stack, 0, unroll=4)
        first_table(f).wait()
        lax.fori_loop(low, high, transform_of(0), 0, unroll=4)
        for hop in range(1, parts):
            pack_for(lax.rem(me + hop, parts), send_ref, f)
            if f == 0 and hop == 1:
                pl.semaphore_wait(barrier, parts + rings - 2)
            first_copy(f, hop, me).start()
        pack_for(me, recv_ref, f)
    for piece, (first, end) in enumerate(out_pieces):
        for chunk in range(first, end):
            table_copy(chunk).wait()
            lax.fori_loop(0, ord_dev, transform_of(chunk), 0, unroll=4)
            for f in range(halves):
                lax.fori_loop(0, 2 * shells, pack_of(chunk, f), 0, unroll=8)
            recv_ref[me, chunk] = send_ref[me, chunk]
        for hop in range(1, parts):
            lat_copy(piece, hop, me).start()

    for copy in small:
        copy.wait()
    offset = nr_total * 7 // 13
    cut = [slice(block * 128, (block + 1) * 128) for block in range(blocks)]
    tile = (full, 128)
    tiles = [(pair, block) for pair in range(pairs) for block in range(blocks)]
    blank = jnp.zeros(tile, jnp.float32)
    unity = jnp.ones(tile, jnp.float32)

    def angular(pair, block):
        degree = (
            me * ord_dev
            + pair * 2 * per
            + block * 128
            + lax.broadcasted_iota(jnp.int32, tile, 0) // 2
            + lax.broadcasted_iota(jnp.int32, tile, 1)
        ).astype(jnp.float32)
        return degree * (degree + 1.0)

    angulars = [angular(pair, block) for pair, block in tiles]

    def factor(shell, carry):
        kappa = jnp.full(tile, kappa_ref[shell], jnp.float32)
        spot = jnp.full(tile, ring * shells + shell, jnp.int32)
        lower = jnp.where(spot > 0, -kappa, 0.0)
        upper = jnp.where(spot < nr_total - 1, -kappa, 0.0)
        radius = (offset + spot).astype(jnp.float32)
        weight = kappa / (radius * radius)
        new = []
        for k, (pair, block) in enumerate(tiles):
            ratio, pull, weighed = carry[k]
            first_ref[pair, shell, :, cut[block]] = weighed
            diagonal = 1.0 + 2.0 * kappa + weight * angulars[k]
            inverse = 1.0 / (diagonal - lower * ratio)
            ratio = upper * inverse
            pull = -lower * pull * inverse
            inverse_ref[pair, shell, :, cut[block]] = inverse
            ratio_ref[pair, shell, :, cut[block]] = ratio
            beta_ref[pair, shell, :, cut[block]] = pull
            new.append((ratio, pull, -ratio * weighed))
        return tuple(new)

    lax.fori_loop(0, shells, factor, tuple((blank, unity, unity) for _ in tiles))

    def unfactor(step, carry):
        shell = shells - 1 - step
        spot = jnp.full(tile, ring * shells + shell, jnp.int32)
        pushed = jnp.where(spot > 0, jnp.full(tile, kappa_ref[shell], jnp.float32), 0.0)
        new = []
        for k, (pair, block) in enumerate(tiles):
            beta, gamma, to_first, to_end = carry[k]
            inverse = inverse_ref[pair, shell, :, cut[block]]
            to_first = inverse * (first_ref[pair, shell, :, cut[block]] + to_first)
            to_end = inverse * to_end
            first_ref[pair, shell, :, cut[block]] = to_first
            end_ref[pair, shell, :, cut[block]] = to_end
            ratio = ratio_ref[pair, shell, :, cut[block]]
            beta = beta_ref[pair, shell, :, cut[block]] - ratio * beta
            gamma = -ratio * gamma
            beta_ref[pair, shell, :, cut[block]] = beta
            gamma_ref[pair, shell, :, cut[block]] = gamma
            new.append((beta, gamma, pushed * to_first, pushed * to_end))
        return tuple(new)

    lax.fori_loop(0, shells, unfactor, tuple((blank, unity, blank, unity) for _ in tiles))
    for pair in range(pairs):
        for side, shell in enumerate((0, shells - 1)):
            slope_ref[2 * side, pair] = beta_ref[pair, shell]
            slope_ref[2 * side + 1, pair] = gamma_ref[pair, shell]
    slopes_ref[ring] = slope_ref[...]
    for hop in range(1, rings):
        slope_copy(hop, ring).start()

    def multiply_of(chunk):
        def back_of(locals_):
            grids = []
            for which in range(2):
                lat = jnp.concatenate(
                    [
                        jnp.concatenate(
                            [
                                recv_ref[part, chunk, f, which, local]
                                for part in range(parts)
                                for f in range(halves)
                            ],
                            axis=0,
                        )
                        for local in locals_
                    ],
                    axis=1,
                )
                grids.append(jnp.dot(synth_ref[...], lat, preferred_element_type=jnp.float32))
            product = (grids[0] * grids[1]).astype(jnp.bfloat16)
            return jnp.dot(analysis_ref[...], product, preferred_element_type=jnp.float32) * scale

        def multiply(step, carry):
            backs = [back_of((step * 4 + 2 * k, step * 4 + 2 * k + 1)) for k in range(2)]
            for part in range(parts):
                for group in range(groups):
                    base = (part * groups + group) * rows
                    back_send_ref[group, part, chunk, step] = jnp.concatenate(
                        [back[base : base + rows, k * width : (k + 1) * width] for back in backs for k in range(2)],
                        axis=0,
                    ).astype(jnp.bfloat16)
            return carry

        return multiply

    for piece in range(-1, len(out_pieces)):
        for hop in range(1, parts):
            for copy in lat_copies(piece, hop, lax.rem(me + parts - hop, parts)):
                copy.wait_recv()
        first, end = (0, 1) if piece < 0 else out_pieces[piece]
        for chunk in range(first, end):
            lax.fori_loop(0, mine // 4, multiply_of(chunk), 0)
        if end >= chunks - 1:
            for group in range(early):
                send_back(group, end - chunks + 1)
    for group in range(early, units[lead - 1][0][-1] + 1):
        for piece in range(len(pieces[group])):
            send_back(group, piece)
    for group in range(groups):
        back_recv_ref[group, me] = back_send_ref[group, me]

    for hop in range(1, rings):
        slope_copy(hop, partner(ring, hop, rings)).wait_recv()
    for pair, block in tiles:
        slope = blank
        for device in range(rings):
            head0, head1, tail0, tail1 = [slopes_ref[device, k, pair, :, cut[block]] for k in range(4)]
            inverse = 1.0 / (1.0 - head0 * slope)
            gain = head1 * inverse
            carried = tail0 * slope * inverse
            for k, value in enumerate((inverse, head0 * inverse, gain, carried, tail0 + carried * head0, slope)):
                chain_ref[pair, device, k, :, cut[block]] = value
            slope = tail1 + tail0 * slope * gain

    def widen(group, part):
        for chunk in range(chunks):
            for step in range(mine // 4):
                base = pl.multiple_of((part * mine + 4 * step) * rows, 4 * rows)
                wide_ref[chunk, pl.ds(base, 4 * rows), :] = back_recv_ref[group, part, chunk, step].astype(
                    jnp.float32
                )

    def untransform(group):
        for local in range(per):
            order = group * per + local
            stacked = jnp.concatenate(
                [
                    jnp.concatenate(
                        [
                            wide_ref[chunk, pl.ds(2 * local + half, shells, stride=rows), :].astype(jnp.bfloat16)
                            for chunk in range(chunks)
                        ],
                        axis=1,
                    )
                    for half in range(2)
                ],
                axis=0,
            )
            table = jnp.concatenate([table_ref[chunk, order] for chunk in range(chunks)], axis=1)
            forcing = lax.dot_general(
                stacked, table, (((1,), (1,)), ((), ())), preferred_element_type=jnp.float32
            )
            for half in range(2):
                right = field_ref[:, order, half, :] + forcing[half * shells : (half + 1) * shells]
                row = (group % 2) * rows + 2 * local + half
                for block in range(blocks):
                    right_ref[block, pl.ds(row, shells, stride=full), :] = right[:, cut[block]]

    def send_edges(unit):
        _, pair, low, high = units[unit]
        size = high - low

        def gather(shell, carry):
            new = []
            for block in range(blocks):
                right = right_ref[block, pl.ds(pl.multiple_of(shell * full, full) + low, size), :]
                for side, weights in enumerate((first_ref, end_ref)):
                    new.append(carry[2 * block + side] + right * weights[pair, shell, low:high, cut[block]])
            return tuple(new)

        zeros = tuple(jnp.zeros((size, 128), jnp.float32) for _ in range(2 * blocks))
        sums = lax.fori_loop(0, shells, gather, zeros, unroll=8)
        here, there = edge_buffers(unit)
        for block in range(blocks):
            for side in range(2):
                here[side * size : (side + 1) * size, cut[block]] = sums[2 * block + side]
        for hop in reversed(range(1, rings)):
            edge_copy(unit, hop, ring).start()
        there[ring] = here[...]

    def solve(unit):
        _, pair, low, high = units[unit]
        empty = tuple(jnp.zeros((high - low, 128), jnp.float32) for _ in range(blocks))

        def forward(shell, carry):
            index = ring * shells + shell
            lower = jnp.where(jnp.full(empty[0].shape, index, jnp.int32) > 0, -kappa_ref[shell], 0.0)
            start = shell * full
            new = []
            for block in range(blocks):
                right = right_ref[block, pl.ds(pl.multiple_of(start, full) + low, high - low), :]
                value = (right - lower * carry[block]) * inverse_ref[pair, shell, low:high, cut[block]]
                alpha_ref[pair, shell, low:high, cut[block]] = value
                new.append(value)
            return tuple(new)

        lax.fori_loop(0, shells, forward, empty, unroll=4)

        def backward(step, carry):
            shell = shells - 1 - step
            new = []
            for block in range(blocks):
                value = (
                    alpha_ref[pair, shell, low:high, cut[block]]
                    - ratio_ref[pair, shell, low:high, cut[block]] * carry[block]
                )
                alpha_ref[pair, shell, low:high, cut[block]] = value
                new.append(value)
            return tuple(new)

        lax.fori_loop(0, shells, backward, empty, unroll=4)
    def finish(unit):
        members, pair, low, high = units[unit]
        size = high - low
        for hop in reversed(range(1, rings)):
            edge_copy(unit, hop, partner(ring, hop, rings)).wait_recv()
        _, there = edge_buffers(unit)
        empty = jnp.zeros((size, 128), jnp.float32)
        spot = jnp.full((size, 128), ring, jnp.int32)
        befores, afters = [], []
        for block in range(blocks):
            known, consts, left, tilt = empty, [], empty, empty
            for device in range(rings):
                first, end = [there[device, side * size : (side + 1) * size, cut[block]] for side in range(2)]
                inverse, headed, _, carried, through, slope = [
                    chain_ref[pair, device, k, low:high, cut[block]] for k in range(6)
                ]
                here = spot == device
                left = jnp.where(here, known, left)
                tilt = jnp.where(here, slope, tilt)
                consts.append(inverse * first + headed * known)
                known = end + carried * first + through * known
            beyond, before, after = empty, empty, empty
            for device in reversed(range(rings)):
                here = spot == device
                start = consts[device] + chain_ref[pair, device, 2, low:high, cut[block]] * beyond
                before = jnp.where(here, left + tilt * start, before)
                after = jnp.where(here, beyond, after)
                beyond = start
            befores.append(before)
            afters.append(after)

        def emit(shell, carry):
            for block in range(blocks):
                value = (
                    alpha_ref[pair, shell, low:high, cut[block]]
                    + beta_ref[pair, shell, low:high, cut[block]] * befores[block]
                    + gamma_ref[pair, shell, low:high, cut[block]] * afters[block]
                )
                for k in range(size // 2):
                    out_ref[shell, members[0] * per + k, :, cut[block]] = value[2 * k : 2 * k + 2]
            return carry

        lax.fori_loop(0, shells, emit, 0, unroll=4)

    def settle(unit):
        for group in units[unit][0]:
            for piece in range(len(pieces[group])):
                for hop in range(1, parts):
                    back_copy(group, piece, hop, me).wait_send()

    for unit, (members, _, _, _) in enumerate(units):
        for group in members:
            if unit == last:
                widen(group, me)
            for piece in range(len(pieces[group])):
                for hop in range(1, parts):
                    back_copy(group, piece, hop, lax.rem(me + parts - hop, parts)).wait_recv()
                    if unit == last:
                        widen(group, lax.rem(me + parts - hop, parts))
        if unit + lead <= last:
            for group in units[unit + lead][0]:
                for piece in range(len(pieces[group])):
                    send_back(group, piece)
        for group in members:
            if unit < last:
                for part in range(parts):
                    widen(group, part)
            untransform(group)
        send_edges(unit)
        solve(unit)
        if unit == 0:
            for hop in range(1, parts):
                for piece in range(-1, len(out_pieces)):
                    for copy in lat_copies(piece, hop, me):
                        copy.wait_send()
            for hop in range(1, rings):
                slope_copy(hop, ring).wait_send()
        else:
            finish(unit - 1)
            settle(unit - 1)
            for hop in range(1, rings):
                edge_copy(unit - 1, hop, ring).wait_send()
    settle(last)
    finish(last)
    for hop in range(1, rings):
        edge_copy(last, hop, ring).wait_send()


def on_device(scalar_field, radial_flow, legendre, diffusivity):
    shells, ord_dev, _, degrees = scalar_field.shape
    lats = legendre.shape[2]
    parts, rings = lax.axis_size("mode"), lax.axis_size("radial")
    mine = shells // parts
    synth, analysis, scale = longitude_tables(ord_dev * parts)
    width, per, orders_half = 128, 2, 8
    chunks, blocks = lats // width, degrees // 128
    halves, groups = ord_dev // orders_half, ord_dev // per
    pairs, full = groups // 2, 4 * per
    assert rings & (rings - 1) == 0 and mine % 4 == 0 and chunks >= 5
    assert lats % width == 0 and degrees % 128 == 0 and ord_dev % orders_half == 0
    bf16, f32 = jnp.bfloat16, jnp.float32
    vmem, hbm = pl.BlockSpec(memory_space=pltpu.VMEM), pl.BlockSpec(memory_space=pltpu.HBM)
    dma = pltpu.SemaphoreType.DMA
    solved = pltpu.VMEM((pairs, shells, full, degrees), f32)
    there = pltpu.VMEM((parts, chunks, halves, 2, mine, 2 * orders_half, width), bf16)
    back = pltpu.VMEM((groups, parts, chunks, mine // 4, 8 * per, width), bf16)
    return pl.pallas_call(
        functools.partial(whole_step, scale),
        in_specs=[hbm] * 6,
        out_specs=vmem,
        out_shape=pltpu.VMEM(scalar_field.shape, f32),
        scratch_shapes=[
            pltpu.SMEM(diffusivity.shape, f32),
            pltpu.VMEM(synth.shape, bf16),
            pltpu.VMEM(analysis.shape, bf16),
            pltpu.VMEM(scalar_field.shape, f32),
            pltpu.VMEM(scalar_field.shape, f32),
            pltpu.VMEM((chunks, ord_dev, degrees, width), bf16),
            pltpu.VMEM((ord_dev, 4 * shells, degrees), bf16),
            pltpu.VMEM((4 * shells * ord_dev, width), f32),
            there, there, back, back,
            pltpu.VMEM((chunks, shells * 2 * per, width), f32),
            pltpu.VMEM((blocks, shells * full, 128), f32),
            solved, solved, solved, solved, solved, solved, solved,
            pltpu.VMEM((4, pairs, full, degrees), f32),
            pltpu.VMEM((rings, 4, pairs, full, degrees), f32),
            pltpu.VMEM((pairs, rings, 6, full, degrees), f32),
            pltpu.VMEM((pairs - 1, 2 * full, degrees), f32),
            pltpu.VMEM((pairs - 1, rings, 2 * full, degrees), f32),
            pltpu.VMEM((2, full, degrees), f32),
            pltpu.VMEM((2, rings, full, degrees), f32),
            dma((3,)),
            dma((2, halves)),
            dma((halves + chunks - 1,)),
            dma((halves + 3, parts - 1)),
            dma((halves + 3, parts - 1)),
            dma((groups + 2, parts - 1)),
            dma((groups + 2, parts - 1)),
            dma((rings - 1,)),
            dma((rings - 1,)),
            dma((pairs + 1, rings - 1)),
            dma((pairs + 1, rings - 1)),
        ],
        compiler_params=params(collective_id=0, has_side_effects=True),
        name="whole_step",
    )(diffusivity, legendre, scalar_field, radial_flow, synth, analysis)


def solution(mesh):
    return jax.shard_map(
        on_device,
        mesh=mesh,
        in_specs=(
            P("radial", "mode", None, None),
            P("radial", "mode", None, None),
            P("mode", None, None),
            P("radial"),
        ),
        out_specs=P("radial", "mode", None, None),
        check_vma=False,
    )
```
